256 devices in a mesh: rep: 16 (over y, z_lo), tp: 8 (over x, core), seq: 2 (over z_hi).
Axes of the slice: x: 4, y: 4, z: 8 (z_hi: 2, z_lo: 4; z = z_hi * 4 + z_lo), core: 2. Of those that a mesh axis runs over, the one named last changes fastest.
Arguments:
- dec_in: bfloat16 [16, 4, 8192], P('rep'), may hold values from -6 to 6
- decode_query: bfloat16 [16, 4, 4096], P('rep'), may hold values from -120 to 120
- cache: bfloat16 [16, 8192, 1024], P('rep', ('tp', 'seq')), may hold values from -6 to 6
- ctx_len: int32 [16], P('rep'), may hold values from 2048 to 8192
- pack_in: bfloat16 [32768, 8192], P(('rep', 'tp', 'seq')), may hold values from -6 to 6
- packed_query: bfloat16 [32768, 4096], P(('rep', 'tp', 'seq')), may hold values from -120 to 120
- seg_ids: int32 [32768], P(('rep', 'tp', 'seq')), may hold values from 0 to 31, never falling along the last dimension, each value on 1 to 2048 neighbouring positions
- norm_gain: float32 [8192], replicated, may hold values from 0.1 to 1.9
- key_value_weight: bfloat16 [8192, 1024], P(('rep', 'tp', 'seq')), may hold values from -0.0625 to 0.0625
Outputs:
- dec_out: bfloat16 [16, 4, 4096], P('rep')
- pack_out: bfloat16 [32768, 4096], P(('rep', 'tp', 'seq'))
The draws below stay inside these ranges and needn't reach their ends.
Inputs may be any that keep to these rules, and one draw needn't show every extreme that they name: seg_ids never falls along the tokens; one response spans at most 2048 consecutive tokens.
All inputs are finite; a program needn't handle non-finite values.
Results may differ from the reference program's by a relative error of at most 0.0085.
Values may be sent and summed in bfloat16 or wider, within the bound.
No kernel may reach another device: no remote copies, remote signals or barrier semaphores. Data moves between devices by JAX's collectives and lax.ppermute only.
A program may use at most 128 MiB of HBM per device.

```python
import math
import jax
import jax.numpy as jnp
import numpy as np
from jax import lax

MODEL_WIDTH = 8192
HEAD_SIZE = 128
QUERY_HEADS = 32
KEY_VALUE_HEADS = 4
DECODE_STEPS = 4
CONTEXT_LIMIT = 8192
DEVICE_TOKENS = 128
ROLLOUT_ROWS = 16
PACK_TOKENS = 2048
TOKENS = 32768


def boosted(key, row_count, cols):
    value_rows = jnp.clip(jax.random.normal(jax.random.fold_in(key, 3), (row_count, cols), jnp.float32), -5.0, 5.0)
    return value_rows


def draw_decode_query(key, part):
    value_rows = boosted(jax.random.fold_in(key, 11), ROLLOUT_ROWS * DECODE_STEPS, QUERY_HEADS * HEAD_SIZE)
    return value_rows.reshape(ROLLOUT_ROWS, DECODE_STEPS, QUERY_HEADS * HEAD_SIZE).astype(jnp.bfloat16)


def draw_packed_query(key, part):
    value_rows = boosted(jax.random.fold_in(key, 23), TOKENS, QUERY_HEADS * HEAD_SIZE)
    return value_rows.astype(jnp.bfloat16)


def with_ends(result, rng, low, largest):
    longest = result.shape.index(max(result.shape))
    spots = []
    for shift in (0, 1):
        where = [jax.random.randint(jax.random.fold_in(rng, axis), (), 0, length) for axis, length in enumerate(result.shape)]
        where[longest] = (where[longest] + shift) % result.shape[longest]
        spots.append(tuple(where))
    return result.at[spots[0]].set(low).at[spots[1]].set(largest)


def block_scale(rng, extent, cuts, low, largest):
    level = 1.0
    for axis_at, parts in cuts:
        draws = jax.random.uniform(jax.random.fold_in(jax.random.fold_in(rng, 6), axis_at), (parts,), jnp.float32, low / len(cuts), largest / len(cuts))
        level = level * jnp.repeat(jnp.exp(draws), extent[axis_at] // parts).reshape((-1,) + (1,) * (len(extent) - 1 - axis_at))
    return level


def length_profile(number_of, total, limit, slope):
    portions = [(1 << 20) // math.isqrt(grade ** slope) + 1 for grade in range(2, number_of + 1)]
    rest, counts = total - limit - (number_of - 1), [1] * (number_of - 1)
    while rest > 0:
        candidates = [i for i in range(number_of - 1) if counts[i] < limit]
        mass, left = sum([portions[i] for i in candidates]), rest
        for i in candidates:
            extra = min(limit - counts[i], max(1, left * portions[i] // mass), rest)
            counts[i] = counts[i] + extra
            rest = rest - extra
    return np.array([limit] + counts)


def ragged_sizes(stream_key, number_of, total, bound, lean):
    if number_of == 2:
        one = jax.random.randint(stream_key, (), max(1, total - bound), min(bound, total - 1) + 1)
        return jnp.stack([one, total - one])
    lengths = jnp.asarray(length_profile(number_of, total, bound, lean), jnp.int32)
    pairs = (number_of - 1) // 2
    source_of, sink = lengths[1:1 + 2 * pairs:2], lengths[2:2 + 2 * pairs:2]
    slack = jnp.minimum(source_of - 1, bound - sink)
    shifted = jax.random.randint(jax.random.fold_in(stream_key, 1), (pairs,), 0, 1 << 20) % (slack + 1)
    lengths = lengths.at[1:1 + 2 * pairs:2].set(source_of - shifted).at[2:2 + 2 * pairs:2].set(sink + shifted)
    return lengths[jax.random.permutation(jax.random.fold_in(stream_key, 2), number_of)]


def gaussian(stream_key, dims, scale, most, pieces=(), kind=jnp.bfloat16):
    values = scale * jax.random.normal(stream_key, dims, jnp.float32)
    if pieces:
        values = values * block_scale(stream_key, dims, pieces, -0.22, 0.18)
    return jnp.clip(values, -most, most).astype(kind)


def setup_inputs(seed: int = 0) -> dict:
    arg_keys = jax.random.split(jax.random.key(seed), 10)
    dec_in = gaussian(arg_keys[0], (ROLLOUT_ROWS, DECODE_STEPS, MODEL_WIDTH), 1.0, 6.0, ((0, 16),))
    decode_query = draw_decode_query(jax.random.fold_in(arg_keys[9], 71), 0)
    cache = gaussian(arg_keys[2], (ROLLOUT_ROWS, CONTEXT_LIMIT, 2 * KEY_VALUE_HEADS * HEAD_SIZE), 1.0, 6.0, ((0, 16), (1, 16)))
    ctx_len = with_ends(jax.random.randint(arg_keys[3], (ROLLOUT_ROWS,), CONTEXT_LIMIT // 4, CONTEXT_LIMIT + 1), jax.random.fold_in(arg_keys[3], 1), CONTEXT_LIMIT // 4, CONTEXT_LIMIT).astype(jnp.int32)
    pack_in = gaussian(arg_keys[4], (TOKENS, MODEL_WIDTH), 1.0, 6.0, ((0, 256),))
    packed_query = draw_packed_query(jax.random.fold_in(arg_keys[9], 71), 0)
    seg_ids = jnp.searchsorted(jnp.cumsum(ragged_sizes(arg_keys[6], 2 * TOKENS // PACK_TOKENS, TOKENS, PACK_TOKENS, 1)), jnp.arange(TOKENS), side="right").astype(jnp.int32)
    norm_gain = jnp.clip(1.0 + 0.18 * jax.random.normal(arg_keys[7], (MODEL_WIDTH,), jnp.float32), 0.1, 1.9)
    key_value_weight = gaussian(arg_keys[8], (MODEL_WIDTH, 2 * KEY_VALUE_HEADS * HEAD_SIZE), MODEL_WIDTH ** -0.5, 0.0625, ((0, 256),))
    return {"dec_in": dec_in, "decode_query": decode_query, "cache": cache, "ctx_len": ctx_len, "pack_in": pack_in, "packed_query": packed_query, "seg_ids": seg_ids, "norm_gain": norm_gain, "key_value_weight": key_value_weight}


def normalize(row_values, gain):
    value_rows = row_values.astype(jnp.float32)
    power = lax.optimization_barrier(jnp.mean(value_rows * value_rows, axis=-1, keepdims=True))
    return value_rows * lax.rsqrt(power + 1e-05) * gain

def attend_heads(query_rows, key_rows, value_rows, attention_mask):
    scores = jnp.einsum('qkgd,pkd->qkgp', query_rows.astype(jnp.float32), key_rows.astype(jnp.float32), precision=lax.Precision.HIGHEST) / math.sqrt(HEAD_SIZE)
    allowed = attention_mask[:, None, None, :]
    scores = jnp.where(allowed, scores, -1e+30)
    top = lax.optimization_barrier(jnp.max(scores, axis=-1, keepdims=True))
    weights = jnp.where(allowed, jnp.exp(scores - top), 0.0)
    total = lax.optimization_barrier(jnp.sum(weights, axis=-1))
    rounded = weights.astype(jnp.bfloat16)
    mixed = jnp.einsum('qkgp,pkd->qkgd', rounded.astype(jnp.float32), value_rows.astype(jnp.float32), precision=lax.Precision.HIGHEST)
    return mixed / total[..., None]

def reference(dec_in, decode_query, cache, ctx_len, pack_in, packed_query, seg_ids, norm_gain, key_value_weight):
    column_width = KEY_VALUE_HEADS * HEAD_SIZE
    query_group = QUERY_HEADS // KEY_VALUE_HEADS
    weight_full = key_value_weight.astype(jnp.float32)
    dec_norm = normalize(dec_in.reshape(ROLLOUT_ROWS * DECODE_STEPS, MODEL_WIDTH), norm_gain)
    decode_key_value = jnp.dot(dec_norm, weight_full, preferred_element_type=jnp.float32, precision=lax.Precision.HIGHEST)
    decode_key_value = decode_key_value.reshape(ROLLOUT_ROWS, DECODE_STEPS, 2 * column_width)
    pack_norm = normalize(pack_in, norm_gain)
    pack_kv = jnp.dot(pack_norm, weight_full, preferred_element_type=jnp.float32, precision=lax.Precision.HIGHEST)
    positions = jnp.arange(CONTEXT_LIMIT + DECODE_STEPS, dtype=jnp.int32)
    step_index = jnp.arange(DECODE_STEPS, dtype=jnp.int32)

    def decode_row(items):
        query_rows, older, newer, length = items
        gathered_keys = jnp.concatenate([older.astype(jnp.float32), newer.astype(jnp.float32)], axis=0)
        key_rows = gathered_keys[:, :column_width].reshape(-1, KEY_VALUE_HEADS, HEAD_SIZE)
        value_rows = gathered_keys[:, column_width:].reshape(-1, KEY_VALUE_HEADS, HEAD_SIZE)
        attention_mask = jnp.where(positions[None, :] < CONTEXT_LIMIT, positions[None, :] < length, positions[None, :] - CONTEXT_LIMIT <= step_index[:, None])
        final_output = attend_heads(query_rows.reshape(DECODE_STEPS, KEY_VALUE_HEADS, query_group, HEAD_SIZE), key_rows, value_rows, attention_mask)
        return final_output.reshape(DECODE_STEPS, QUERY_HEADS * HEAD_SIZE).astype(jnp.bfloat16)
    dec_out = lax.map(decode_row, (decode_query, cache, decode_key_value, ctx_len))
    pack_list = TOKENS // PACK_TOKENS
    token_extent = PACK_TOKENS // DEVICE_TOKENS
    kv_packs = pack_kv.reshape(pack_list, PACK_TOKENS, 2 * column_width)
    seg_packs = seg_ids.reshape(pack_list, PACK_TOKENS)
    packed_query_rows = packed_query.reshape(pack_list, token_extent, DEVICE_TOKENS, KEY_VALUE_HEADS, query_group, HEAD_SIZE)
    key_pos = jnp.arange(PACK_TOKENS, dtype=jnp.int32)
    block_index = jnp.arange(token_extent, dtype=jnp.int32)

    def pack_group(items):
        queries, single_key_value, seg_one = items
        key_rows = single_key_value[:, :column_width].reshape(PACK_TOKENS, KEY_VALUE_HEADS, HEAD_SIZE)
        value_rows = single_key_value[:, column_width:].reshape(PACK_TOKENS, KEY_VALUE_HEADS, HEAD_SIZE)

        def query_block(inner):
            query_rows, index = inner
            first = (index * DEVICE_TOKENS).astype(jnp.int32)
            query_pos = first + jnp.arange(DEVICE_TOKENS, dtype=jnp.int32)
            segs = lax.dynamic_slice_in_dim(seg_one, first, DEVICE_TOKENS)
            attention_mask = (seg_one[None, :] == segs[:, None]) & (key_pos[None, :] <= query_pos[:, None])
            final_output = attend_heads(query_rows, key_rows, value_rows, attention_mask)
            return final_output.reshape(DEVICE_TOKENS, QUERY_HEADS * HEAD_SIZE).astype(jnp.bfloat16)
        return lax.map(query_block, (queries, block_index))
    pack_out = lax.map(pack_group, (packed_query_rows, kv_packs, seg_packs))
    return (dec_out, pack_out.reshape(TOKENS, QUERY_HEADS * HEAD_SIZE))
```

```python
import functools
import math

import jax
import jax.numpy as jnp
from jax import lax
from jax.experimental import pallas as pl
from jax.experimental.pallas import tpu as pltpu
from jax.sharding import Mesh
from jax.sharding import PartitionSpec as P

WIDTH = 8192
HEAD = 128
STEPS = 4
CHUNK = 128
SLICE = 2048
MESSAGE = SLICE + 128
ROWS = 4 * CHUNK + 16
FACTOR = math.log2(math.e) / math.sqrt(HEAD)
SCALE = 1.0 / math.sqrt(HEAD)
LOW = -1e30

f32 = jnp.float32
bf16 = jnp.bfloat16


VMEM = pl.BlockSpec(memory_space=pltpu.VMEM)
SMEM = pl.BlockSpec(memory_space=pltpu.SMEM)


def call(body, outs, inputs, smem=1, scratch=(), name=None):
    return pl.pallas_call(
        body,
        out_shape=outs,
        in_specs=[SMEM] * smem + [VMEM] * (len(inputs) - smem),
        out_specs=jax.tree.map(lambda _: VMEM, outs),
        scratch_shapes=list(scratch),
        compiler_params=pltpu.CompilerParams(vmem_limit_bytes=56 * 1024 * 1024),
        name=name,
    )(*inputs)


def sds(shape, dtype):
    return jax.ShapeDtypeStruct(shape, dtype)


def aligned(value, multiple):
    return pl.multiple_of(value, multiple)


def norm_columns(ref, rows):
    power = jnp.zeros((rows, 128), f32)
    for block in range(WIDTH // 128):
        piece = ref[:, block * 128 : (block + 1) * 128].astype(f32)
        power = power + piece * piece
    mean = jnp.sum(power, axis=1, keepdims=True) * (1.0 / WIDTH)
    factor = lax.rsqrt(mean + 1e-05)
    high = factor.astype(bf16).astype(f32)
    middle = (factor - high).astype(bf16).astype(f32)
    low = factor - high - middle
    lane = lax.broadcasted_iota(jnp.int32, (rows, 128), 1)
    packed = jnp.where(
        lane == 0, high, jnp.where(lane == 1, middle, jnp.where(lane == 2, low, 0.0))
    )
    return packed.astype(bf16)


def prepare_kernel(at, pack, query, dec, *outs):
    x = at[2]
    messages, queries, dec_message = outs[:4], outs[4:8], outs[8]
    columns = norm_columns(pack, CHUNK)
    for shift in range(4):
        target = (x + shift) & 3
        for block in range(16):
            start = aligned(block * 512 + target * 128, 128)
            messages[shift][:, block * 128 : (block + 1) * 128] = pack[:, pl.ds(start, 128)]
        messages[shift][:, SLICE:] = columns
        queries[shift][...] = query[:, pl.ds(aligned(target * 1024, 128), 1024)]
    for block in range(16):
        start = aligned(block * 512 + x * 128, 128)
        dec_message[:, block * 128 : (block + 1) * 128] = dec[:, pl.ds(start, 128)]
    dec_message[:, SLICE:] = norm_columns(dec, 16)


def cache_kernel(at, length, query, cache, *rest):
    outs, rows = rest[:4], rest[4]
    x, chunk = at[2], at[2] * 4 + at[3] * 2 + at[4]
    local = cache.shape[0]
    for shift in range(4):
        head = (x + shift) & 3
        for group in range(8):
            start = aligned(head * 1024 + group * 128, 128)
            rows[group * 4 : group * 4 + 4, :] = query[:, pl.ds(start, 128)].astype(f32)
        q = rows[...].astype(bf16)
        keys = cache[:, pl.ds(aligned(head * 128, 128), 128)]
        values = cache[:, pl.ds(aligned(512 + head * 128, 128), 128)]
        scores = lax.dot_general(q, keys, (((1,), (1,)), ((), ())), preferred_element_type=f32)
        where = chunk * local + lax.broadcasted_iota(jnp.int32, scores.shape, 1)
        allowed = where < length[0]
        scores = jnp.where(allowed, scores * SCALE, LOW)
        top = jnp.max(scores, axis=1, keepdims=True)
        weights = jnp.where(allowed, jnp.exp(scores - top), 0.0)
        total = jnp.sum(weights, axis=1, keepdims=True)
        mixed = jnp.dot(weights.astype(bf16), values, preferred_element_type=f32)
        outs[shift][0:32, :] = mixed
        outs[shift][32:64, :] = jnp.broadcast_to(top, (32, 128))
        outs[shift][64:96, :] = jnp.broadcast_to(total, (32, 128))


def project_kernel(at, x0, x1, x2, x3, dec, gain, here, there, *rest):
    outs, inputs, weights, product, result = rest[:4], rest[4], rest[5], rest[6], rest[7]
    y, z, x, c, s = at[0], at[1], at[2], at[3], at[4]
    for jy in range(4):
        for jz in range(4):
            block = (((y - jy) & 3) * 4 + ((z - jz) & 3)) * 128
            for js in range(2):
                source = (jy * 4 + jz) * 64 + js * 32
                place = block + (s ^ js) * 32
                weights[pl.ds(aligned(place + c * 64, 32), 32), :] = here[source : source + 32, :]
                weights[pl.ds(aligned(place + (1 - c) * 64, 32), 32), :] = there[
                    source : source + 32, :
                ]
    pieces = [(x0, x & 3, CHUNK), (x1, (x - 1) & 3, CHUNK), (x2, (x - 2) & 3, CHUNK)]
    pieces += [(x3, (x - 3) & 3, CHUNK), (dec, 4, 16)]
    for block in range(16):
        columns = slice(block * 128, (block + 1) * 128)
        factor = gain[:, pl.ds(aligned(block * 512 + x * 128, 128), 128)]
        for ref, position, count in pieces:
            start = position * CHUNK
            value = ref[:, columns].astype(f32) * factor
            high = value.astype(bf16)
            inputs[pl.ds(aligned(start, 16), count), columns] = high
            inputs[pl.ds(aligned(start + ROWS, 16), count), columns] = (
                value - high.astype(f32)
            ).astype(bf16)
    product[...] = jnp.dot(inputs[...], weights[...], preferred_element_type=f32)
    for ref, position, count in pieces:
        start = position * CHUNK
        factor = jnp.sum(ref[:, SLICE:].astype(f32), axis=1, keepdims=True)
        rows = pl.ds(aligned(start, 16), count)
        result[rows, :] = (
            product[rows, :] + product[pl.ds(aligned(start + ROWS, 16), count), :]
        ) * factor
    for shift in range(4):
        head = (x + shift) & 3
        outs[shift][...] = result[:, pl.ds(aligned(head * 128, 128), 128)].astype(
            outs[shift].dtype
        )


def total_kernel(k0, k1, k2, k3, v0, v1, v2, v3, slab, dec_key, dec_value):
    key = (k0[...] + k1[...]) + (k2[...] + k3[...])
    value = (v0[...] + v1[...].astype(f32)) + (v2[...].astype(f32) + v3[...].astype(f32))
    high = key.astype(bf16)
    low = (key - high.astype(f32)).astype(bf16)
    slab[:, 0:128] = high[: 4 * CHUNK]
    slab[:, 128:256] = low[: 4 * CHUNK]
    slab[:, 256:384] = value[: 4 * CHUNK].astype(bf16)
    dec_key[...] = key[4 * CHUNK :]
    dec_value[...] = value[4 * CHUNK :]


def attend_kernel(
    shift, at, seg_at, query, own, other_s, other_c, other_both, segs, out, slabs, q, top, total, mixed
):
    x, c, s = at[2], at[3], at[4]
    place = c * 2 + s
    chunk = (x + shift) & 3
    for pair, (first, second) in enumerate(((own, other_c), (other_s, other_both))):
        for a in range(4):
            slabs[pair * 4 + a, 0:128, :] = first[a * 128 : (a + 1) * 128, :]
            slabs[pair * 4 + a, 128:256, :] = second[a * 128 : (a + 1) * 128, :]
    for group in range(8):
        piece = query[:, group * 128 : (group + 1) * 128]
        q[group * 128 : (group + 1) * 128, 0:128] = piece
        q[group * 128 : (group + 1) * 128, 128:256] = piece
    top[...] = jnp.full(top.shape, LOW, f32)
    total[...] = jnp.zeros(total.shape, f32)
    mixed[...] = jnp.zeros(mixed.shape, f32)
    rows = lax.broadcasted_iota(jnp.int32, (128, 128), 0)
    lanes = lax.broadcasted_iota(jnp.int32, (128, 128), 1)
    seg_row = segs[pl.ds((x - chunk) & 3, 1), :]
    seg_column = jnp.sum(
        jnp.where(rows == lanes, jnp.broadcast_to(seg_row, (128, 128)), 0), axis=1, keepdims=True
    )
    first_seg = seg_at[(x - chunk) & 3, 0]

    def bias(a, source, where):
        seg = segs[pl.ds(source * 4 + ((x - a) & 3), 1), :]
        allowed = (seg_column == seg) & (
            a * 512 + where * 128 + lanes <= chunk * 512 + place * 128 + rows
        )
        return jnp.where(allowed, 0.0, LOW)

    def block(pair, a):
        index = pair * 4 + a
        left = bias(a, pair, place ^ pair)
        right = bias(a, pair + 2, place ^ (pair + 2))
        keys = slabs[index, :, 0:256]
        values = slabs[index, :, 256:384]
        scores = lax.dot_general(
            q[...], keys, (((1,), (1,)), ((), ())), preferred_element_type=f32
        )
        score_left = (scores[:, 0:128].reshape(8, 128, 128) + left[None]).reshape(1024, 128)
        score_right = (scores[:, 128:256].reshape(8, 128, 128) + right[None]).reshape(1024, 128)
        highest = jnp.max(jnp.maximum(score_left, score_right), axis=1, keepdims=True)
        before = top[...]
        after = jnp.maximum(before, highest)
        fade = jnp.exp2((before - after) * FACTOR)
        weight_left = jnp.exp2((score_left - after) * FACTOR)
        weight_right = jnp.exp2((score_right - after) * FACTOR)
        top[...] = after
        total[...] = total[...] * fade + (weight_left + weight_right)
        weights = jnp.concatenate([weight_left.astype(bf16), weight_right.astype(bf16)], axis=1)
        mixed[...] = mixed[...] * fade + jnp.dot(weights, values, preferred_element_type=f32)

    block(0, chunk)

    def step(index, carry):
        pair, a = index // 4, index % 4
        relative = (x - a) & 3
        last_seg = jnp.maximum(
            seg_at[pair * 4 + relative, 127], seg_at[(pair + 2) * 4 + relative, 127]
        )
        earlier = (a < chunk) | ((a == chunk) & (pair == 1) & (place > 0))

        @pl.when(earlier & (last_seg >= first_seg))
        def _():
            block(pair, a)

        return carry

    lax.fori_loop(0, 8, step, 0)
    sums = jnp.sum(total[...], axis=1, keepdims=True)
    for group in range(8):
        piece = slice(group * 128, (group + 1) * 128)
        out[:, piece] = (mixed[piece, :] / sums[piece, :]).astype(bf16)


def rollout_kernel(at, query, cached, key, value, out, rows):
    head = at[2]
    for group in range(8):
        start = aligned(head * 1024 + group * 128, 128)
        rows[group * 4 : group * 4 + 4, :] = query[:, pl.ds(start, 128)].astype(f32)
    q = rows[...]
    step = lax.broadcasted_iota(jnp.int32, (32, 128), 0) & 3
    scores = []
    for j in range(STEPS):
        score = jnp.sum(q * key[j : j + 1, :], axis=1, keepdims=True) * SCALE
        scores.append(jnp.where(step >= j, jnp.broadcast_to(score, (32, 128)), LOW))
    mixed, top, total = cached[0:32, :], cached[32:64, :], cached[64:96, :]
    high = top
    for score in scores:
        high = jnp.maximum(high, score)
    fade = jnp.exp(top - high)
    mixed, total = mixed * fade, total * fade
    for j, score in enumerate(scores):
        weight = jnp.where(step >= j, jnp.exp(score - high), 0.0)
        total = total + weight
        mixed = mixed + weight.astype(bf16).astype(f32) * value[j : j + 1, :]
    rows[...] = mixed / total
    for group in range(8):
        out[:, group * 128 : (group + 1) * 128] = rows[group * 4 : group * 4 + 4, :].astype(bf16)


def arrange_kernel(at, p0, p1, p2, p3, d0, d1, d2, d3, pack, dec):
    x = at[2]
    for shift, (part, piece) in enumerate(((p0, d0), (p1, d1), (p2, d2), (p3, d3))):
        start = aligned(((x - shift) & 3) * 1024, 128)
        pack[:, pl.ds(start, 1024)] = part[...]
        dec[:, pl.ds(start, 1024)] = piece[...]


def merged(first, second):
    top = jnp.maximum(first[32:64], second[32:64])
    one = jnp.exp(first[32:64] - top)
    two = jnp.exp(second[32:64] - top)
    return jnp.concatenate(
        [
            first[0:32] * one + second[0:32] * two,
            top,
            first[64:96] * one + second[64:96] * two,
        ],
        axis=0,
    )


def moved(value, axis, shift):
    size = 2 if axis in ("c", "s") else 4
    return lax.ppermute(value, axis, [(i, (i + shift) % size) for i in range(size)])


def gathered(value):
    value = jnp.concatenate([value, moved(value, "s", 1)], axis=0)
    value = jnp.concatenate([value] + [moved(value, "zl", i) for i in (1, 2, 3)], axis=0)
    value = jnp.concatenate([value] + [moved(value, "y", i) for i in (1, 2, 3)], axis=0)
    return value, moved(value, "c", 1)


def shards(
    dec_in,
    decode_query,
    cache,
    ctx_len,
    pack_in,
    packed_query,
    seg_ids,
    norm_gain,
    key_value_weight,
):
    at = jnp.stack([lax.axis_index(name) for name in ("y", "zl", "x", "c", "s")]).astype(jnp.int32)
    dec_rows = jnp.pad(dec_in[0], ((0, 12), (0, 0)))
    dec_query = decode_query[0]
    prepared = call(
        prepare_kernel,
        [sds((CHUNK, MESSAGE), bf16)] * 4 + [sds((CHUNK, 1024), bf16)] * 4 + [sds((16, MESSAGE), bf16)],
        (at, pack_in, packed_query, dec_rows),
        name="prepare",
    )
    messages, queries, dec_message = prepared[:4], prepared[4:8], prepared[8]
    weights = [gathered(key_value_weight[:, :512]), gathered(key_value_weight[:, 512:])]
    inputs = [messages[0]] + [moved(messages[i], "x", i) for i in (1, 2, 3)]

    seg_row = seg_ids.reshape(1, CHUNK)
    segs = jnp.concatenate([seg_row] + [moved(seg_row, "x", i) for i in (1, 2, 3)], axis=0)
    segs = jnp.concatenate([segs, moved(segs, "s", 1)], axis=0)
    segs = jnp.concatenate([segs, moved(segs, "c", 1)], axis=0)

    cached = call(
        cache_kernel,
        [sds((96, 128), f32)] * 4,
        (at, ctx_len, dec_query, cache[0]),
        smem=2,
        scratch=[pltpu.VMEM((32, 128), f32)],
        name="cached",
    )
    state = cached[0]
    for i in (1, 2, 3):
        state = merged(state, moved(cached[i], "x", i))
    state = merged(state, moved(state, "c", 1))
    state = merged(state, moved(state, "s", 1))

    query_parts = [queries[0]] + [moved(queries[i], "x", i) for i in (1, 2, 3)]

    gain = norm_gain.reshape(1, WIDTH)

    def projected(weight, kind):
        outs = call(
            project_kernel,
            [sds((ROWS, 128), f32)] + [sds((ROWS, 128), kind)] * 3,
            (at, *inputs, dec_message, gain, *weight),
            scratch=[
                pltpu.VMEM((2 * ROWS, SLICE), bf16),
                pltpu.VMEM((SLICE, 512), bf16),
                pltpu.VMEM((2 * ROWS, 512), f32),
                pltpu.VMEM((ROWS, 512), f32),
            ],
            name="project",
        )
        return [outs[0]] + [moved(outs[i], "x", i) for i in (1, 2, 3)]

    keys = projected(weights[0], f32)
    values = projected(weights[1], bf16)
    slab, dec_key, dec_value = call(
        total_kernel,
        [sds((4 * CHUNK, 384), bf16), sds((16, 128), f32), sds((16, 128), f32)],
        (*keys, *values),
        smem=0,
        name="total",
    )
    slab_s = moved(slab, "s", 1)
    slab_c = moved(slab, "c", 1)
    slab_both = moved(slab_s, "c", 1)

    rollout = call(
        rollout_kernel,
        sds((STEPS, 1024), bf16),
        (at, dec_query, state, dec_key, dec_value),
        scratch=[pltpu.VMEM((32, 128), f32)],
        name="rollout",
    )
    rollouts = [rollout] + [moved(rollout, "x", i) for i in (1, 2, 3)]

    parts = [None] * 4
    for shift in (1, 2, 3, 0):
        part = call(
            functools.partial(attend_kernel, shift),
            sds((CHUNK, 1024), bf16),
            (at, segs, query_parts[(4 - shift) % 4], slab, slab_s, slab_c, slab_both, segs),
            smem=2,
            scratch=[
                pltpu.VMEM((8, 256, 384), bf16),
                pltpu.VMEM((1024, 256), bf16),
                pltpu.VMEM((1024, 128), f32),
                pltpu.VMEM((1024, 128), f32),
                pltpu.VMEM((1024, 128), f32),
            ],
            name=f"attend{shift}",
        )
        parts[shift] = part if shift == 0 else moved(part, "x", shift)
    pack_out, dec_out = call(
        arrange_kernel,
        [sds((CHUNK, 4096), bf16), sds((STEPS, 4096), bf16)],
        (at, *parts, *rollouts),
        name="arrange",
    )
    return dec_out[None], pack_out


def solution(mesh):
    grid = Mesh(mesh.devices.reshape(4, 4, 4, 2, 2), ("y", "zl", "x", "c", "s"))
    rep = ("y", "zl")
    rest = ("x", "c", "s")
    placed = (
        P(rep, None, None),
        P(rep, None, None),
        P(rep, rest, None),
        P(rep),
        P(rep + rest, None),
        P(rep + rest, None),
        P(rep + rest),
        P(),
        P(rep + rest, None),
    )
    return jax.shard_map(
        shards,
        mesh=grid,
        in_specs=placed,
        out_specs=(P(rep, None, None), P(rep + rest, None)),
        check_vma=False,
    )
```

```python
import functools
import math

import jax
import jax.numpy as jnp
from jax import lax
from jax.experimental import pallas as pl
from jax.experimental.pallas import tpu as pltpu
from jax.sharding import Mesh
from jax.sharding import PartitionSpec as P


WIDTH = 8192
HEAD = 128
STEPS = 4
CHUNK = 128
SLICE = 2048
MESSAGE = SLICE + 128
ROWS = 4 * CHUNK + 16
FACTOR = math.log2(math.e) / math.sqrt(HEAD)
SCALE = 1.0 / math.sqrt(HEAD)
LOW = -1e30

f32 = jnp.float32
bf16 = jnp.bfloat16


VMEM = pl.BlockSpec(memory_space=pltpu.VMEM)
SMEM = pl.BlockSpec(memory_space=pltpu.SMEM)


def call(body, outs, inputs, smem=1, scratch=()):
    inputs = [
        value if i < smem else pltpu.with_memory_space_constraint(value, pltpu.VMEM)
        for i, value in enumerate(inputs)
    ]
    return pl.pallas_call(
        body,
        out_shape=outs,
        in_specs=[SMEM] * smem + [VMEM] * (len(inputs) - smem),
        out_specs=jax.tree.map(lambda _: VMEM, outs),
        scratch_shapes=list(scratch),
        compiler_params=pltpu.CompilerParams(vmem_limit_bytes=32 * 1024 * 1024),
    )(*inputs)


def sds(shape, dtype):
    return jax.ShapeDtypeStruct(shape, dtype)


def aligned(value, multiple):
    return pl.multiple_of(value, multiple)


def columns_of(ref, rows, seg):
    power = jnp.zeros((rows, 128), f32)
    for block in range(WIDTH // 128):
        piece = ref[:, block * 128 : (block + 1) * 128].astype(f32)
        power = power + piece * piece
    mean = jnp.sum(power, axis=1, keepdims=True) * (1.0 / WIDTH)
    factor = lax.rsqrt(mean + 1e-05)
    high, middle, low = thirds(factor)
    lane = lax.broadcasted_iota(jnp.int32, (rows, 128), 1)
    packed = jnp.where(
        lane == 0, high, jnp.where(lane == 1, middle, jnp.where(lane == 2, low, 0.0))
    )
    if seg is not None:
        packed = jnp.where(lane == 3, seg, packed)
    return packed.astype(bf16)


def thirds(value):
    high = value.astype(bf16).astype(f32)
    middle = (value - high).astype(bf16).astype(f32)
    return high, middle, value - high - middle


def diagonal():
    rows = lax.broadcasted_iota(jnp.int32, (128, 128), 0)
    return rows == lax.broadcasted_iota(jnp.int32, (128, 128), 1)


def column_of(row):
    spread = jnp.broadcast_to(row, (128, 128))
    return jnp.sum(jnp.where(diagonal(), spread, 0.0), axis=1, keepdims=True)


def prepare_kernel(at, pack, seg, rollout, *outs):
    x = at[2]
    messages, dec_message, dec = outs[:4], outs[4], outs[5]
    dec[...] = jnp.zeros(dec.shape, f32)
    dec[0:STEPS, :] = rollout[...].astype(f32)
    columns = columns_of(pack, CHUNK, column_of(seg[...].astype(f32)))
    for shift in range(4):
        target = (x + shift) & 3
        for block in range(16):
            start = aligned(block * 512 + target * 128, 128)
            messages[shift][:, block * 128 : (block + 1) * 128] = pack[:, pl.ds(start, 128)]
        messages[shift][:, SLICE:] = columns
    for block in range(16):
        start = aligned(block * 512 + x * 128, 128)
        dec_message[:, block * 128 : (block + 1) * 128] = dec[:, pl.ds(start, 128)].astype(bf16)
    dec_message[:, SLICE:] = columns_of(dec, 16, None)


def cache_kernel(at, length, query, cache, packed, *rest):
    outs, rows = rest[:4], rest[4]
    x, chunk = at[2], at[2] * 4 + at[3] * 2 + at[4]
    local = cache.shape[0]
    for shift in range(4):
        head = (x + shift) & 3
        out = outs[shift]
        out[0:CHUNK, :] = packed[:, pl.ds(aligned(head * 1024, 128), 1024)]
        for group in range(8):
            start = aligned(head * 1024 + group * 128, 128)
            rows[group * 4 : group * 4 + 4, :] = query[:, pl.ds(start, 128)].astype(f32)
        q = rows[...].astype(bf16)
        keys = cache[:, pl.ds(aligned(head * 128, 128), 128)]
        values = cache[:, pl.ds(aligned(512 + head * 128, 128), 128)]
        scores = lax.dot_general(q, keys, (((1,), (1,)), ((), ())), preferred_element_type=f32)
        where = chunk * local + lax.broadcasted_iota(jnp.int32, scores.shape, 1)
        allowed = where < length[0]
        scores = jnp.where(allowed, scores * SCALE, LOW)
        top = jnp.max(scores, axis=1, keepdims=True)
        weights = jnp.where(allowed, jnp.exp(scores - top), 0.0)
        total = jnp.sum(weights, axis=1, keepdims=True)
        mixed = jnp.dot(weights.astype(bf16), values, preferred_element_type=f32)
        wide = (mixed, jnp.broadcast_to(top, (32, 128)), jnp.broadcast_to(total, (32, 128)))
        for which, value in enumerate(wide):
            for third, piece in enumerate(thirds(value)):
                start = CHUNK + 16 * third
                for half in range(2):
                    lanes = slice((which * 2 + half) * 128, (which * 2 + half + 1) * 128)
                    out[start : start + 16, lanes] = piece[16 * half : 16 * half + 16].astype(bf16)
        out[CHUNK:, 768:] = jnp.zeros((48, 256), bf16)


def joined(parts):
    top = functools.reduce(jnp.maximum, [part[1] for part in parts])
    mixed, total = jnp.zeros_like(top), jnp.zeros_like(top)
    for part in parts:
        fade = jnp.exp(part[1] - top)
        mixed = mixed + part[0] * fade
        total = total + part[2] * fade
    return mixed, top, total


def shared(refs):
    parts = []
    for ref in refs:
        values = []
        for which in range(3):
            halves = []
            for half in range(2):
                lanes = slice((which * 2 + half) * 128, (which * 2 + half + 1) * 128)
                tail = ref[CHUNK:, lanes].astype(f32)
                halves.append(tail[0:16] + tail[16:32] + tail[32:48])
            values.append(jnp.concatenate(halves, axis=0))
        parts.append(values)
    return jnp.concatenate(joined(parts), axis=0)


def state_of(slab):
    parts = [slab[ROWS + 48 * third : ROWS + 48 * third + 48, :].astype(f32) for third in range(3)]
    both = parts[0] + parts[1] + parts[2]
    state = jnp.concatenate([both[:, 0:128], both[:, 128:256]], axis=0)
    return [state[32 * which : 32 * which + 32] for which in range(3)]


def project_kernel(for_keys, at, x0, x1, x2, x3, dec, gain, here, there, *rest):
    outs, (inputs, weights, product, result) = rest[:-4], rest[-4:]
    y, z, x, c, s = at[0], at[1], at[2], at[3], at[4]
    for jy in range(4):
        for jz in range(4):
            block = (((y - jy) & 3) * 4 + ((z - jz) & 3)) * 128
            for js in range(2):
                source = (jy * 4 + jz) * 64 + js * 32
                place = block + (s ^ js) * 32
                weights[pl.ds(aligned(place + c * 64, 32), 32), :] = here[source : source + 32, :]
                weights[pl.ds(aligned(place + (1 - c) * 64, 32), 32), :] = there[
                    source : source + 32, :
                ]
    pieces = [(x0, x & 3, CHUNK), (x1, (x - 1) & 3, CHUNK), (x2, (x - 2) & 3, CHUNK)]
    pieces += [(x3, (x - 3) & 3, CHUNK), (dec, 4, 16)]
    for block in range(16):
        columns = slice(block * 128, (block + 1) * 128)
        factor = gain[:, pl.ds(aligned(block * 512 + x * 128, 128), 128)]
        for ref, position, count in pieces:
            start = position * CHUNK
            value = ref[:, columns].astype(f32) * factor
            high = value.astype(bf16)
            inputs[pl.ds(aligned(start, 16), count), columns] = high
            if for_keys:
                inputs[pl.ds(aligned(start + ROWS, 16), count), columns] = (
                    value - high.astype(f32)
                ).astype(bf16)
    product[...] = jnp.dot(inputs[...], weights[...], preferred_element_type=f32)
    for ref, position, count in pieces:
        start = position * CHUNK
        tail = ref[:, SLICE:].astype(f32)
        lane = lax.broadcasted_iota(jnp.int32, tail.shape, 1)
        factor = jnp.sum(jnp.where(lane < 3, tail, 0.0), axis=1, keepdims=True)
        rows = pl.ds(aligned(start, 16), count)
        value = product[rows, :]
        if for_keys:
            value = value + product[pl.ds(aligned(start + ROWS, 16), count), :]
        result[rows, :] = value * factor
    for shift in range(4):
        head = (x + shift) & 3
        outs[shift][...] = result[:, pl.ds(aligned(head * 128, 128), 128)].astype(
            outs[shift].dtype
        )
    if for_keys:
        outs[4][...] = jnp.zeros((16, 128), f32)
        for ref, position, _ in pieces[:4]:
            tail = ref[:, SLICE:].astype(f32)
            lane = lax.broadcasted_iota(jnp.int32, tail.shape, 1)
            seg = jnp.sum(jnp.where(lane == 3, tail, 0.0), axis=1, keepdims=True)
            spread = jnp.broadcast_to(seg, (128, 128))
            outs[4][pl.ds(position, 1), :] = jnp.sum(
                jnp.where(diagonal(), spread, 0.0), axis=0, keepdims=True
            )


def keys_kernel(k0, k1, k2, k3, seg, q0, q1, q2, q3, slab, dec_key):
    for third, piece in enumerate(thirds(shared((q0, q1, q2, q3)))):
        rows = slice(ROWS + 48 * third, ROWS + 48 * third + 48)
        slab[rows, 0:128] = piece[0:48].astype(bf16)
        slab[rows, 128:256] = piece[48:96].astype(bf16)
    key = (k0[...] + k1[...]) + (k2[...] + k3[...])
    scaled = key[: 4 * CHUNK] * FACTOR
    high = scaled.astype(bf16)
    slab[0 : 4 * CHUNK, 0:128] = high
    slab[0 : 4 * CHUNK, 128:256] = (scaled - high.astype(f32)).astype(bf16)
    slab[4 * CHUNK : ROWS, 0:128] = seg[...].astype(bf16)
    slab[4 * CHUNK : ROWS, 128:256] = jnp.zeros((16, 128), bf16)
    dec_key[...] = key[4 * CHUNK :]


def values_kernel(v0, v1, v2, v3, slab, dec_value):
    value = (v0[...] + v1[...].astype(f32)) + (v2[...].astype(f32) + v3[...].astype(f32))
    slab[...] = value[: 4 * CHUNK].astype(bf16)
    dec_value[...] = value[4 * CHUNK :]


def load_keys(keys, values, slabs, segs, ends):
    for side in range(2):
        for a in range(4):
            rows, chunk = slice(side * 128, side * 128 + 128), slice(a * 128, a * 128 + 128)
            slabs[a, rows, 0:256] = keys[side][chunk, :]
            slabs[a, rows, 256:384] = values[side][chunk, :]
        segs[16 * side : 16 * side + 16, :] = keys[side][4 * CHUNK : ROWS, 0:128].astype(f32)
    for a in range(4):
        ends[a] = jnp.max(jnp.maximum(segs[a : a + 1, :], segs[16 + a : 17 + a, :]))


def double(query, q):
    for group in range(8):
        piece = query[0:CHUNK, group * 128 : (group + 1) * 128]
        q[group * 128 : (group + 1) * 128, 0:128] = piece
        q[group * 128 : (group + 1) * 128, 128:256] = piece


def attend(a, chunk, place, pair, column, q, slabs, segs, top, total, mixed):
    keys = slabs[a, :, 0:256]
    values = slabs[a, :, 256:384]
    scores = lax.dot_general(q[...], keys, (((1,), (1,)), ((), ())), preferred_element_type=f32)
    rows = lax.broadcasted_iota(jnp.int32, (128, 128), 0)
    lanes = lax.broadcasted_iota(jnp.int32, (128, 128), 1)

    def hidden(score, side):
        seg = segs[pl.ds(16 * side + a, 1), :]
        where = place ^ (pair + 2 * side)
        allowed = (column == seg) & (
            a * 512 + where * 128 + lanes <= chunk * 512 + place * 128 + rows
        )
        bias = jnp.where(allowed, 0.0, LOW)
        return (score.reshape(8, 128, 128) + bias[None]).reshape(1024, 128)

    left, right = hidden(scores[:, 0:128], 0), hidden(scores[:, 128:256], 1)
    highest = jnp.max(jnp.maximum(left, right), axis=1, keepdims=True)
    before = top[...]
    after = jnp.maximum(before, highest)
    fade = jnp.exp2(before - after)
    left = jnp.exp2(left - after)
    right = jnp.exp2(right - after)
    top[...] = after
    total[...] = total[...] * fade + (left + right)
    weights = jnp.concatenate([left.astype(bf16), right.astype(bf16)], axis=1)
    mixed[...] = mixed[...] * fade + jnp.dot(weights, values, preferred_element_type=f32)


def near_kernel(
    at, q0, q1, q2, q3, own, other_c, own_value, other_value, seg,
    top, total, mixed, slabs, q, segs, ends,
):
    x, place = at[2], at[3] * 2 + at[4]
    load_keys((own, other_c), (own_value, other_value), slabs, segs, ends)
    for shift, query in enumerate((q0, q3, q2, q1)):
        double(query, q.at[shift])
    top[...] = jnp.full(top.shape, LOW, f32)
    total[...] = jnp.zeros(total.shape, f32)
    mixed[...] = jnp.zeros(mixed.shape, f32)

    def query_chunk(shift, carry):
        chunk = (x + shift) & 3
        row = seg[pl.ds(chunk, 1), :]
        column = column_of(row)
        first = jnp.min(row)
        state = (q.at[shift], slabs, segs, top.at[shift], total.at[shift], mixed.at[shift])

        def step(back, inner):
            a = chunk - back

            @pl.when((back == 0) | (ends[a] >= first))
            def _():
                attend(a, chunk, place, 0, column, *state)

            return inner

        lax.fori_loop(0, chunk + 1, step, 0)
        return carry

    lax.fori_loop(0, 4, query_chunk, 0)


def far_kernel(
    shift, at, query, other_s, other_both, value_s, value_both, seg, rollout, top0, total0, mixed0,
    out, slabs, q, segs, ends, top, total, mixed,
):
    x, place = at[2], at[3] * 2 + at[4]
    chunk = (x + shift) & 3
    load_keys((other_s, other_both), (value_s, value_both), slabs, segs, ends)
    double(query, q)
    top[...] = top0[shift]
    total[...] = total0[shift]
    mixed[...] = mixed0[shift]
    row = seg[pl.ds(chunk, 1), :]
    column = column_of(row)
    first = jnp.min(row)
    state = (q, slabs, segs, top, total, mixed)

    def step(a, carry):
        @pl.when(((a < chunk) | (place > 0)) & (ends[a] >= first))
        def _():
            attend(a, chunk, place, 1, column, *state)

        return carry

    lax.fori_loop(0, chunk + 1, step, 0)
    sums = jnp.sum(total[...], axis=1, keepdims=True)
    for group in range(8):
        piece = slice(group * 128, (group + 1) * 128)
        out[0:CHUNK, piece] = (mixed[piece, :] / sums[piece, :]).astype(bf16)
    out[CHUNK:, :] = rollout[...]


def rollout_kernel(at, query, s0, s1, s2, s3, key, value, out, rows):
    head = at[2]
    for group in range(8):
        start = aligned(head * 1024 + group * 128, 128)
        rows[group * 4 : group * 4 + 4, :] = query[:, pl.ds(start, 128)].astype(f32)
    q = rows[...]
    step = lax.broadcasted_iota(jnp.int32, (32, 128), 0) & 3
    scores = []
    for j in range(STEPS):
        score = jnp.sum(q * key[j : j + 1, :], axis=1, keepdims=True) * SCALE
        scores.append(jnp.where(step >= j, jnp.broadcast_to(score, (32, 128)), LOW))
    mixed, top, total = joined([state_of(slab) for slab in (s0, s1, s2, s3)])
    high = functools.reduce(jnp.maximum, scores, top)
    fade = jnp.exp(top - high)
    mixed, total = mixed * fade, total * fade
    for j, score in enumerate(scores):
        weight = jnp.where(step >= j, jnp.exp(score - high), 0.0)
        total = total + weight
        mixed = mixed + weight.astype(bf16).astype(f32) * value[j : j + 1, :]
    rows[...] = mixed / total
    out[...] = jnp.zeros(out.shape, bf16)
    for group in range(8):
        out[0:4, group * 128 : (group + 1) * 128] = rows[group * 4 : group * 4 + 4, :].astype(bf16)


def arrange_kernel(at, p0, p1, p2, p3, pack, dec):
    x = at[2]
    for shift, part in enumerate((p0, p1, p2, p3)):
        start = aligned(((x - shift) & 3) * 1024, 128)
        pack[:, pl.ds(start, 1024)] = part[0:CHUNK, :]
        dec[:, pl.ds(start, 1024)] = part[CHUNK : CHUNK + STEPS, :]


def moved(value, axis, shift):
    size = 2 if axis in ("c", "s") else 4
    return lax.ppermute(value, axis, [(i, (i + shift) % size) for i in range(size)])


def around(values, axis):
    return [values[0]] + [moved(values[i], axis, i) for i in (1, 2, 3)]


def layer(
    dec_in,
    decode_query,
    cache,
    ctx_len,
    pack_in,
    packed_query,
    seg_ids,
    norm_gain,
    key_value_weight,
):
    at = jnp.stack([lax.axis_index(name) for name in ("y", "zl", "x", "c", "s")]).astype(jnp.int32)
    dec_query = decode_query[0]
    gain = norm_gain.reshape(1, WIDTH)

    weight = jnp.concatenate([key_value_weight, moved(key_value_weight, "s", 1)], axis=0)
    *messages, dec_message = call(
        prepare_kernel,
        [sds((CHUNK, MESSAGE), bf16)] * 4 + [sds((16, MESSAGE), bf16)],
        (at, pack_in, seg_ids.reshape(1, CHUNK), dec_in[0]),
        scratch=[pltpu.VMEM((16, WIDTH), f32)],
    )
    inputs = around(messages, "x")
    weight = jnp.concatenate(around([weight] * 4, "zl"), axis=0)
    cached = call(
        cache_kernel,
        [sds((CHUNK + 48, 1024), bf16)] * 4,
        (at, ctx_len, dec_query, cache[0], packed_query),
        smem=2,
        scratch=[pltpu.VMEM((32, 128), f32)],
    )
    queries = around(cached, "x")

    def gathered(part):
        part = jnp.concatenate(around([part] * 4, "y"), axis=0)
        return part, moved(part, "c", 1)

    key_weight = gathered(weight[:, :512])
    value_weight = gathered(weight[:, 512:])

    def projected(part, kind, form):
        for_keys = kind == "k"
        height = 2 * ROWS if for_keys else ROWS
        outs = call(
            functools.partial(project_kernel, for_keys),
            [sds((ROWS, 128), f32)]
            + [sds((ROWS, 128), form)] * 3
            + [sds((16, 128), f32)] * for_keys,
            (at, *inputs, dec_message, gain, *part),
            scratch=[
                pltpu.VMEM((height, SLICE), bf16),
                pltpu.VMEM((SLICE, 512), bf16),
                pltpu.VMEM((height, 512), f32),
                pltpu.VMEM((ROWS, 512), f32),
            ],
        )
        return around(outs[:4], "x"), outs[4:]

    keys, (seg,) = projected(key_weight, "k", f32)
    values, _ = projected(value_weight, "v", bf16)

    key, dec_key = call(
        keys_kernel,
        [sds((ROWS + 144, 256), bf16), sds((16, 128), f32)],
        (*keys, seg, *queries),
        smem=0,
    )
    key_s = moved(key, "s", 1)
    key_c = moved(key, "c", 1)
    value, dec_value = call(
        values_kernel, [sds((4 * CHUNK, 128), bf16), sds((16, 128), f32)], values, smem=0
    )
    value_s = moved(value, "s", 1)
    value_c = moved(value, "c", 1)
    slots = [
        pltpu.VMEM((4, 256, 384), bf16),
        pltpu.VMEM((4, 1024, 256), bf16),
        pltpu.VMEM((32, 128), f32),
        pltpu.SMEM((4,), f32),
    ]
    running = call(
        near_kernel,
        [sds((4, 1024, 128), f32)] * 3,
        (at, *queries, key, key_c, value, value_c, seg),
        scratch=slots,
    )
    key_both = moved(key_s, "c", 1)
    value_both = moved(value_s, "c", 1)
    rollout = call(
        rollout_kernel,
        sds((16, 1024), bf16),
        (at, dec_query, key, key_s, key_c, key_both, dec_key, dec_value),
        scratch=[pltpu.VMEM((32, 128), f32)],
    )
    slots[1] = pltpu.VMEM((1024, 256), bf16)
    parts = [None] * 4
    for shift in (2, 1, 3, 0):
        part = call(
            functools.partial(far_kernel, shift),
            sds((CHUNK + 16, 1024), bf16),
            (
                at, queries[(4 - shift) % 4], key_s, key_both, value_s, value_both, seg, rollout,
                *running,
            ),
            scratch=slots + [pltpu.VMEM((1024, 128), f32)] * 3,
        )
        parts[shift] = part if shift == 0 else moved(part, "x", shift)
    pack_out, dec_out = call(
        arrange_kernel, [sds((CHUNK, 4096), bf16), sds((STEPS, 4096), bf16)], (at, *parts)
    )
    return dec_out[None], pack_out


def solution(mesh):
    grid = Mesh(mesh.devices.reshape(4, 4, 4, 2, 2), ("y", "zl", "x", "c", "s"))
    rep = ("y", "zl")
    rest = ("x", "c", "s")
    placed = (
        P(rep, None, None),
        P(rep, None, None),
        P(rep, rest, None),
        P(rep),
        P(rep + rest, None),
        P(rep + rest, None),
        P(rep + rest),
        P(),
        P(rep + rest, None),
    )
    return jax.shard_map(
        layer,
        mesh=grid,
        in_specs=placed,
        out_specs=(P(rep, None, None), P(rep + rest, None)),
        check_vma=False,
    )
```

```python
import functools
import math

import jax
import jax.numpy as jnp
from jax import lax
from jax.experimental import pallas as pl
from jax.experimental.pallas import tpu as pltpu
from jax.sharding import Mesh
from jax.sharding import PartitionSpec as P


WIDTH = 8192
HEAD = 128
STEPS = 4
CHUNK = 128
SLICE = 2048
MESSAGE = SLICE + 128
ROWS = 4 * CHUNK + 16
FACTOR = math.log2(math.e) / math.sqrt(HEAD)
SCALE = 1.0 / math.sqrt(HEAD)
LOW = -1e30

f32 = jnp.float32
bf16 = jnp.bfloat16


VMEM = pl.BlockSpec(memory_space=pltpu.VMEM)
SMEM = pl.BlockSpec(memory_space=pltpu.SMEM)


def call(body, outs, inputs, smem=1, scratch=()):
    inputs = [
        value if i < smem else pltpu.with_memory_space_constraint(value, pltpu.VMEM)
        for i, value in enumerate(inputs)
    ]
    return pl.pallas_call(
        body,
        out_shape=outs,
        in_specs=[SMEM] * smem + [VMEM] * (len(inputs) - smem),
        out_specs=jax.tree.map(lambda _: VMEM, outs),
        scratch_shapes=list(scratch),
        compiler_params=pltpu.CompilerParams(vmem_limit_bytes=32 * 1024 * 1024),
    )(*inputs)


def sds(shape, dtype):
    return jax.ShapeDtypeStruct(shape, dtype)


def aligned(value, multiple):
    return pl.multiple_of(value, multiple)


def columns_of(ref, rows, seg):
    power = jnp.zeros((rows, 128), f32)
    for block in range(WIDTH // 128):
        piece = ref[:, block * 128 : (block + 1) * 128].astype(f32)
        power = power + piece * piece
    mean = jnp.sum(power, axis=1, keepdims=True) * (1.0 / WIDTH)
    factor = lax.rsqrt(mean + 1e-05)
    high, middle, low = thirds(factor)
    lane = lax.broadcasted_iota(jnp.int32, (rows, 128), 1)
    packed = jnp.where(
        lane == 0, high, jnp.where(lane == 1, middle, jnp.where(lane == 2, low, 0.0))
    )
    if seg is not None:
        packed = jnp.where(lane == 3, seg, packed)
    return packed.astype(bf16)


def thirds(value):
    high = value.astype(bf16).astype(f32)
    middle = (value - high).astype(bf16).astype(f32)
    return high, middle, value - high - middle


def diagonal():
    rows = lax.broadcasted_iota(jnp.int32, (128, 128), 0)
    return rows == lax.broadcasted_iota(jnp.int32, (128, 128), 1)


def column_of(row):
    spread = jnp.broadcast_to(row, (128, 128))
    return jnp.sum(jnp.where(diagonal(), spread, 0.0), axis=1, keepdims=True)


def prepare_kernel(at, pack, seg, rollout, *outs):
    x = at[2]
    messages, dec_message, dec = outs[:4], outs[4], outs[5]
    dec[...] = jnp.zeros(dec.shape, f32)
    dec[0:STEPS, :] = rollout[...].astype(f32)
    columns = columns_of(pack, CHUNK, column_of(seg[...].astype(f32)))
    for shift in range(4):
        target = (x + shift) & 3
        for block in range(16):
            start = aligned(block * 512 + target * 128, 128)
            messages[shift][:, block * 128 : (block + 1) * 128] = pack[:, pl.ds(start, 128)]
        messages[shift][:, SLICE:] = columns
    for block in range(16):
        start = aligned(block * 512 + x * 128, 128)
        dec_message[:, block * 128 : (block + 1) * 128] = dec[:, pl.ds(start, 128)].astype(bf16)
    dec_message[:, SLICE:] = columns_of(dec, 16, None)


def cache_kernel(at, length, query, cache, packed, *rest):
    outs, rows = rest[:4], rest[4]
    x, chunk = at[2], at[2] * 4 + at[3] * 2 + at[4]
    local = cache.shape[0]
    for shift in range(4):
        head = (x + shift) & 3
        out = outs[shift]
        out[0:CHUNK, :] = packed[:, pl.ds(aligned(head * 1024, 128), 1024)]
        for group in range(8):
            start = aligned(head * 1024 + group * 128, 128)
            rows[group * 4 : group * 4 + 4, :] = query[:, pl.ds(start, 128)].astype(f32)
        q = rows[...].astype(bf16)
        keys = cache[:, pl.ds(aligned(head * 128, 128), 128)]
        values = cache[:, pl.ds(aligned(512 + head * 128, 128), 128)]
        scores = lax.dot_general(q, keys, (((1,), (1,)), ((), ())), preferred_element_type=f32)
        where = chunk * local + lax.broadcasted_iota(jnp.int32, scores.shape, 1)
        allowed = where < length[0]
        scores = jnp.where(allowed, scores * SCALE, LOW)
        top = jnp.max(scores, axis=1, keepdims=True)
        weights = jnp.where(allowed, jnp.exp(scores - top), 0.0)
        total = jnp.sum(weights, axis=1, keepdims=True)
        mixed = jnp.dot(weights.astype(bf16), values, preferred_element_type=f32)
        wide = (mixed, jnp.broadcast_to(top, (32, 128)), jnp.broadcast_to(total, (32, 128)))
        for which, value in enumerate(wide):
            for third, piece in enumerate(thirds(value)):
                start = CHUNK + 16 * third
                for half in range(2):
                    lanes = slice((which * 2 + half) * 128, (which * 2 + half + 1) * 128)
                    out[start : start + 16, lanes] = piece[16 * half : 16 * half + 16].astype(bf16)
        out[CHUNK:, 768:] = jnp.zeros((48, 256), bf16)


def joined(parts):
    top = functools.reduce(jnp.maximum, [part[1] for part in parts])
    mixed, total = jnp.zeros_like(top), jnp.zeros_like(top)
    for part in parts:
        fade = jnp.exp(part[1] - top)
        mixed = mixed + part[0] * fade
        total = total + part[2] * fade
    return mixed, top, total


def shared(refs):
    parts = []
    for ref in refs:
        values = []
        for which in range(3):
            halves = []
            for half in range(2):
                lanes = slice((which * 2 + half) * 128, (which * 2 + half + 1) * 128)
                tail = ref[CHUNK:, lanes].astype(f32)
                halves.append(tail[0:16] + tail[16:32] + tail[32:48])
            values.append(jnp.concatenate(halves, axis=0))
        parts.append(values)
    return jnp.concatenate(joined(parts), axis=0)


def state_kernel(q0, q1, q2, q3, out):
    out[...] = shared((q0, q1, q2, q3))


def project_kernel(for_keys, at, x0, x1, x2, x3, dec, gain, here, there, *rest):
    outs, (inputs, weights, product, result) = rest[:-4], rest[-4:]
    y, z, x, c, s = at[0], at[1], at[2], at[3], at[4]

    def arrange_weights(jy, carry):
        for jz in range(4):
            block = (((y - jy) & 3) * 4 + ((z - jz) & 3)) * 128
            for js in range(2):
                source = pl.ds(aligned(jy * 256 + jz * 64 + js * 32, 32), 32)
                place = block + (s ^ js) * 32
                weights[pl.ds(aligned(place + c * 64, 32), 32), :] = here[source, :]
                weights[pl.ds(aligned(place + (1 - c) * 64, 32), 32), :] = there[source, :]
        return carry

    lax.fori_loop(0, 4, arrange_weights, 0)
    pieces = [(x0, x & 3, CHUNK), (x1, (x - 1) & 3, CHUNK), (x2, (x - 2) & 3, CHUNK)]
    pieces += [(x3, (x - 3) & 3, CHUNK), (dec, 4, 16)]
    for block in range(16):
        columns = slice(block * 128, (block + 1) * 128)
        factor = gain[:, pl.ds(aligned(block * 512 + x * 128, 128), 128)]
        for ref, position, count in pieces:
            start = position * CHUNK
            value = ref[:, columns].astype(f32) * factor
            high = value.astype(bf16)
            inputs[pl.ds(aligned(start, 16), count), columns] = high
            if for_keys:
                inputs[pl.ds(aligned(start + ROWS, 16), count), columns] = (
                    value - high.astype(f32)
                ).astype(bf16)
    product[...] = jnp.dot(inputs[...], weights[...], preferred_element_type=f32)
    for ref, position, count in pieces:
        start = position * CHUNK
        tail = ref[:, SLICE:].astype(f32)
        lane = lax.broadcasted_iota(jnp.int32, tail.shape, 1)
        factor = jnp.sum(jnp.where(lane < 3, tail, 0.0), axis=1, keepdims=True)
        rows = pl.ds(aligned(start, 16), count)
        value = product[rows, :]
        if for_keys:
            value = value + product[pl.ds(aligned(start + ROWS, 16), count), :]
        result[rows, :] = value * factor
    for shift in range(4):
        head = (x + shift) & 3
        outs[shift][...] = result[:, pl.ds(aligned(head * 128, 128), 128)].astype(
            outs[shift].dtype
        )
    if for_keys:
        outs[4][...] = jnp.zeros((16, 128), f32)
        for ref, position, _ in pieces[:4]:
            tail = ref[:, SLICE:].astype(f32)
            lane = lax.broadcasted_iota(jnp.int32, tail.shape, 1)
            seg = jnp.sum(jnp.where(lane == 3, tail, 0.0), axis=1, keepdims=True)
            spread = jnp.broadcast_to(seg, (128, 128))
            outs[4][pl.ds(position, 1), :] = jnp.sum(
                jnp.where(diagonal(), spread, 0.0), axis=0, keepdims=True
            )


def keys_kernel(k0, k1, k2, k3, seg, slab, dec_key):
    key = (k0[...] + k1[...]) + (k2[...] + k3[...])
    scaled = key[: 4 * CHUNK] * FACTOR
    high = scaled.astype(bf16)
    slab[0 : 4 * CHUNK, 0:128] = high
    slab[0 : 4 * CHUNK, 128:256] = (scaled - high.astype(f32)).astype(bf16)
    slab[4 * CHUNK : ROWS, 0:128] = seg[...].astype(bf16)
    slab[4 * CHUNK : ROWS, 128:256] = jnp.zeros((16, 128), bf16)
    dec_key[...] = key[4 * CHUNK :]


def values_kernel(v0, v1, v2, v3, slab, dec_value):
    value = (v0[...] + v1[...].astype(f32)) + (v2[...].astype(f32) + v3[...].astype(f32))
    slab[...] = value[: 4 * CHUNK].astype(bf16)
    dec_value[...] = value[4 * CHUNK :]


def load_keys(keys, values, slabs, segs, ends):
    for side in range(2):
        for a in range(4):
            rows, chunk = slice(side * 128, side * 128 + 128), slice(a * 128, a * 128 + 128)
            slabs[a, rows, 0:256] = keys[side][chunk, :]
            slabs[a, rows, 256:384] = values[side][chunk, :]
        segs[16 * side : 16 * side + 16, :] = keys[side][4 * CHUNK : ROWS, 0:128].astype(f32)
    for a in range(4):
        ends[a] = jnp.max(jnp.maximum(segs[a : a + 1, :], segs[16 + a : 17 + a, :]))


def double(query, q):
    for group in range(8):
        piece = query[0:CHUNK, group * 128 : (group + 1) * 128]
        q[group * 128 : (group + 1) * 128, 0:128] = piece
        q[group * 128 : (group + 1) * 128, 128:256] = piece


def attend(a, chunk, place, pair, column, q, slabs, segs, top, total, mixed):
    keys = slabs[a, :, 0:256]
    values = slabs[a, :, 256:384]
    scores = lax.dot_general(q[...], keys, (((1,), (1,)), ((), ())), preferred_element_type=f32)
    rows = lax.broadcasted_iota(jnp.int32, (128, 128), 0)
    lanes = lax.broadcasted_iota(jnp.int32, (128, 128), 1)

    def hidden(score, side):
        seg = segs[pl.ds(16 * side + a, 1), :]
        where = place ^ (pair + 2 * side)
        allowed = (column == seg) & (
            a * 512 + where * 128 + lanes <= chunk * 512 + place * 128 + rows
        )
        bias = jnp.where(allowed, 0.0, LOW)
        return (score.reshape(8, 128, 128) + bias[None]).reshape(1024, 128)

    left, right = hidden(scores[:, 0:128], 0), hidden(scores[:, 128:256], 1)
    highest = jnp.max(jnp.maximum(left, right), axis=1, keepdims=True)
    before = top[...]
    after = jnp.maximum(before, highest)
    fade = jnp.exp2(before - after)
    left = jnp.exp2(left - after)
    right = jnp.exp2(right - after)
    top[...] = after
    total[...] = total[...] * fade + (left + right)
    weights = jnp.concatenate([left.astype(bf16), right.astype(bf16)], axis=1)
    mixed[...] = mixed[...] * fade + jnp.dot(weights, values, preferred_element_type=f32)


def near_kernel(
    at, q0, q1, q2, q3, own, other_c, own_value, other_value, seg,
    top, total, mixed, slabs, q, segs, ends,
):
    x, place = at[2], at[3] * 2 + at[4]
    load_keys((own, other_c), (own_value, other_value), slabs, segs, ends)
    for shift, query in enumerate((q0, q3, q2, q1)):
        double(query, q.at[shift])
    top[...] = jnp.full(top.shape, LOW, f32)
    total[...] = jnp.zeros(total.shape, f32)
    mixed[...] = jnp.zeros(mixed.shape, f32)

    def query_chunk(shift, carry):
        chunk = (x + shift) & 3
        row = seg[pl.ds(chunk, 1), :]
        column = column_of(row)
        first = jnp.min(row)
        state = (q.at[shift], slabs, segs, top.at[shift], total.at[shift], mixed.at[shift])

        def step(back, inner):
            a = chunk - back

            @pl.when((back == 0) | (ends[a] >= first))
            def _():
                attend(a, chunk, place, 0, column, *state)

            return inner

        lax.fori_loop(0, chunk + 1, step, 0)
        return carry

    lax.fori_loop(0, 4, query_chunk, 0)


def far_kernel(
    shift, at, query, other_s, other_both, value_s, value_both, seg, rollout, top0, total0, mixed0,
    out, slabs, q, segs, ends, top, total, mixed,
):
    x, place = at[2], at[3] * 2 + at[4]
    chunk = (x + shift) & 3
    load_keys((other_s, other_both), (value_s, value_both), slabs, segs, ends)
    double(query, q)
    top[...] = top0[shift]
    total[...] = total0[shift]
    mixed[...] = mixed0[shift]
    row = seg[pl.ds(chunk, 1), :]
    column = column_of(row)
    first = jnp.min(row)
    state = (q, slabs, segs, top, total, mixed)

    def step(a, carry):
        @pl.when(((a < chunk) | (place > 0)) & (ends[a] >= first))
        def _():
            attend(a, chunk, place, 1, column, *state)

        return carry

    lax.fori_loop(0, chunk + 1, step, 0)
    sums = jnp.sum(total[...], axis=1, keepdims=True)
    for group in range(8):
        piece = slice(group * 128, (group + 1) * 128)
        out[0:CHUNK, piece] = (mixed[piece, :] / sums[piece, :]).astype(bf16)
    out[CHUNK:, :] = rollout[...]


def rollout_kernel(at, query, s0, s1, s2, s3, key, value, out, rows):
    head = at[2]
    for group in range(8):
        start = aligned(head * 1024 + group * 128, 128)
        rows[group * 4 : group * 4 + 4, :] = query[:, pl.ds(start, 128)].astype(f32)
    q = rows[...]
    step = lax.broadcasted_iota(jnp.int32, (32, 128), 0) & 3
    scores = []
    for j in range(STEPS):
        score = jnp.sum(q * key[j : j + 1, :], axis=1, keepdims=True) * SCALE
        scores.append(jnp.where(step >= j, jnp.broadcast_to(score, (32, 128)), LOW))
    mixed, top, total = joined(
        [[ref[32 * i : 32 * i + 32, :] for i in range(3)] for ref in (s0, s1, s2, s3)]
    )
    high = functools.reduce(jnp.maximum, scores, top)
    fade = jnp.exp(top - high)
    mixed, total = mixed * fade, total * fade
    for j, score in enumerate(scores):
        weight = jnp.where(step >= j, jnp.exp(score - high), 0.0)
        total = total + weight
        mixed = mixed + weight.astype(bf16).astype(f32) * value[j : j + 1, :]
    rows[...] = mixed / total
    out[...] = jnp.zeros(out.shape, bf16)
    for group in range(8):
        out[0:4, group * 128 : (group + 1) * 128] = rows[group * 4 : group * 4 + 4, :].astype(bf16)


def arrange_kernel(at, p0, p1, p2, p3, pack, dec):
    x = at[2]
    for shift, part in enumerate((p0, p1, p2, p3)):
        start = aligned(((x - shift) & 3) * 1024, 128)
        pack[:, pl.ds(start, 1024)] = part[0:CHUNK, :]
        dec[:, pl.ds(start, 1024)] = part[CHUNK : CHUNK + STEPS, :]


def moved(value, axis, shift):
    size = 2 if axis in ("c", "s") else 4
    return lax.ppermute(value, axis, [(i, (i + shift) % size) for i in range(size)])


def around(values, axis):
    return [values[0]] + [moved(values[i], axis, i) for i in (1, 2, 3)]


def layer(
    dec_in,
    decode_query,
    cache,
    ctx_len,
    pack_in,
    packed_query,
    seg_ids,
    norm_gain,
    key_value_weight,
):
    at = jnp.stack([lax.axis_index(name) for name in ("y", "zl", "x", "c", "s")]).astype(jnp.int32)
    dec_query = decode_query[0]
    gain = norm_gain.reshape(1, WIDTH)

    weight = jnp.concatenate([key_value_weight, moved(key_value_weight, "s", 1)], axis=0)
    *messages, dec_message = call(
        prepare_kernel,
        [sds((CHUNK, MESSAGE), bf16)] * 4 + [sds((16, MESSAGE), bf16)],
        (at, pack_in, seg_ids.reshape(1, CHUNK), dec_in[0]),
        scratch=[pltpu.VMEM((16, WIDTH), f32)],
    )
    inputs = around(messages, "x")
    cached = call(
        cache_kernel,
        [sds((CHUNK + 48, 1024), bf16)] * 4,
        (at, ctx_len, dec_query, cache[0], packed_query),
        smem=2,
        scratch=[pltpu.VMEM((32, 128), f32)],
    )
    queries = around(cached, "x")

    def gathered(part):
        part = jnp.concatenate(around([part] * 4, "zl"), axis=0)
        part = jnp.concatenate(around([part] * 4, "y"), axis=0)
        return part, moved(part, "c", 1)

    key_weight = gathered(weight[:, :512])
    value_weight = gathered(weight[:, 512:])

    def projected(part, kind, form):
        for_keys = kind == "k"
        height = 2 * ROWS if for_keys else ROWS
        outs = call(
            functools.partial(project_kernel, for_keys),
            [sds((ROWS, 128), f32)]
            + [sds((ROWS, 128), form)] * 3
            + [sds((16, 128), f32)] * for_keys,
            (at, *inputs, dec_message, gain, *part),
            scratch=[
                pltpu.VMEM((height, SLICE), bf16),
                pltpu.VMEM((SLICE, 512), bf16),
                pltpu.VMEM((height, 512), f32),
                pltpu.VMEM((ROWS, 512), f32),
            ],
        )
        return around(outs[:4], "x"), outs[4:]

    keys, (seg,) = projected(key_weight, "k", f32)
    values, _ = projected(value_weight, "v", bf16)

    state = call(state_kernel, sds((96, 128), f32), queries, smem=0)
    state_s = moved(state, "s", 1)
    states = [state, state_s, moved(state, "c", 1), moved(state_s, "c", 1)]

    key, dec_key = call(
        keys_kernel, [sds((ROWS, 256), bf16), sds((16, 128), f32)], (*keys, seg), smem=0
    )
    key_s = moved(key, "s", 1)
    key_c = moved(key, "c", 1)
    value, dec_value = call(
        values_kernel, [sds((4 * CHUNK, 128), bf16), sds((16, 128), f32)], values, smem=0
    )
    value_s = moved(value, "s", 1)
    value_c = moved(value, "c", 1)
    slots = [
        pltpu.VMEM((4, 256, 384), bf16),
        pltpu.VMEM((4, 1024, 256), bf16),
        pltpu.VMEM((32, 128), f32),
        pltpu.SMEM((4,), f32),
    ]
    running = call(
        near_kernel,
        [sds((4, 1024, 128), f32)] * 3,
        (at, *queries, key, key_c, value, value_c, seg),
        scratch=slots,
    )
    key_both = moved(key_s, "c", 1)
    value_both = moved(value_s, "c", 1)
    rollout = call(
        rollout_kernel,
        sds((8, 1024), bf16),
        (at, dec_query, *states, dec_key, dec_value),
        scratch=[pltpu.VMEM((32, 128), f32)],
    )
    slots[1] = pltpu.VMEM((1024, 256), bf16)
    parts = [None] * 4
    for shift in (2, 1, 3, 0):
        part = call(
            functools.partial(far_kernel, shift),
            sds((CHUNK + 8, 1024), bf16),
            (
                at, queries[(4 - shift) % 4], key_s, key_both, value_s, value_both, seg, rollout,
                *running,
            ),
            scratch=slots + [pltpu.VMEM((1024, 128), f32)] * 3,
        )
        parts[shift] = part if shift == 0 else moved(part, "x", shift)
    pack_out, dec_out = call(
        arrange_kernel, [sds((CHUNK, 4096), bf16), sds((STEPS, 4096), bf16)], (at, *parts)
    )
    return dec_out[None], pack_out


def solution(mesh):
    grid = Mesh(mesh.devices.reshape(4, 4, 4, 2, 2), ("y", "zl", "x", "c", "s"))
    rep = ("y", "zl")
    rest = ("x", "c", "s")
    placed = (
        P(rep, None, None),
        P(rep, None, None),
        P(rep, rest, None),
        P(rep),
        P(rep + rest, None),
        P(rep + rest, None),
        P(rep + rest),
        P(),
        P(rep + rest, None),
    )
    return jax.shard_map(
        layer,
        mesh=grid,
        in_specs=placed,
        out_specs=(P(rep, None, None), P(rep + rest, None)),
        check_vma=False,
    )
```

```python
import functools
import math

import jax
import jax.numpy as jnp
from jax import lax
from jax.experimental import pallas as pl
from jax.experimental.pallas import tpu as pltpu
from jax.sharding import Mesh
from jax.sharding import PartitionSpec as P


WIDTH = 8192
HEAD = 128
STEPS = 4
CHUNK = 128
SLICE = 2048
MESSAGE = SLICE + 128
ROWS = 4 * CHUNK + 16
FACTOR = math.log2(math.e) / math.sqrt(HEAD)
SCALE = 1.0 / math.sqrt(HEAD)
LOW = -1e30

f32 = jnp.float32
bf16 = jnp.bfloat16


VMEM = pl.BlockSpec(memory_space=pltpu.VMEM)
SMEM = pl.BlockSpec(memory_space=pltpu.SMEM)


def call(body, outs, inputs, smem=1, scratch=()):
    inputs = [
        value if i < smem else pltpu.with_memory_space_constraint(value, pltpu.VMEM)
        for i, value in enumerate(inputs)
    ]
    return pl.pallas_call(
        body,
        out_shape=outs,
        in_specs=[SMEM] * smem + [VMEM] * (len(inputs) - smem),
        out_specs=jax.tree.map(lambda _: VMEM, outs),
        scratch_shapes=list(scratch),
        compiler_params=pltpu.CompilerParams(vmem_limit_bytes=32 * 1024 * 1024),
    )(*inputs)


def sds(shape, dtype):
    return jax.ShapeDtypeStruct(shape, dtype)


def aligned(value, multiple):
    return pl.multiple_of(value, multiple)


def columns_of(ref, rows, seg):
    power = jnp.zeros((rows, 128), f32)

    def add(group, power):
        for part in range(8):
            piece = ref[:, pl.ds(aligned((group * 8 + part) * 128, 128), 128)].astype(f32)
            power = power + piece * piece
        return power

    power = lax.fori_loop(0, WIDTH // 1024, add, power)
    mean = jnp.sum(power, axis=1, keepdims=True) * (1.0 / WIDTH)
    factor = lax.rsqrt(mean + 1e-05)
    high, middle, low = thirds(factor)
    lane = lax.broadcasted_iota(jnp.int32, (rows, 128), 1)
    packed = jnp.where(
        lane == 0, high, jnp.where(lane == 1, middle, jnp.where(lane == 2, low, 0.0))
    )
    if seg is not None:
        packed = jnp.where(lane == 3, seg, packed)
    return packed.astype(bf16)


def thirds(value):
    high = value.astype(bf16).astype(f32)
    middle = (value - high).astype(bf16).astype(f32)
    return high, middle, value - high - middle


def diagonal():
    rows = lax.broadcasted_iota(jnp.int32, (128, 128), 0)
    return rows == lax.broadcasted_iota(jnp.int32, (128, 128), 1)


def column_of(row):
    spread = jnp.broadcast_to(row, (128, 128))
    return jnp.sum(jnp.where(diagonal(), spread, 0.0), axis=1, keepdims=True)


def prepare_kernel(at, pack, seg, rollout, *outs):
    x = at[2]
    messages, dec_message, dec = outs[:4], outs[4], outs[5]
    dec[...] = jnp.zeros(dec.shape, f32)
    dec[0:STEPS, :] = rollout[...].astype(f32)
    columns = columns_of(pack, CHUNK, column_of(seg[...].astype(f32)))
    for shift in range(4):
        target = (x + shift) & 3
        for block in range(16):
            start = aligned(block * 512 + target * 128, 128)
            messages[shift][:, block * 128 : (block + 1) * 128] = pack[:, pl.ds(start, 128)]
        messages[shift][:, SLICE:] = columns
    for block in range(16):
        start = aligned(block * 512 + x * 128, 128)
        dec_message[:, block * 128 : (block + 1) * 128] = dec[:, pl.ds(start, 128)].astype(bf16)
    dec_message[:, SLICE:] = columns_of(dec, 16, None)


def cache_kernel(at, length, query, cache, packed, *rest):
    outs, states, rows = rest[:4], rest[4:8], rest[8]
    x, chunk = at[2], at[2] * 4 + at[3] * 2 + at[4]
    local = cache.shape[0]
    for shift in range(4):
        head = (x + shift) & 3
        out = outs[shift]
        out[...] = packed[:, pl.ds(aligned(head * 1024, 128), 1024)]
        for group in range(8):
            start = aligned(head * 1024 + group * 128, 128)
            rows[group * 4 : group * 4 + 4, :] = query[:, pl.ds(start, 128)].astype(f32)
        q = rows[...].astype(bf16)
        keys = cache[:, pl.ds(aligned(head * 128, 128), 128)]
        values = cache[:, pl.ds(aligned(512 + head * 128, 128), 128)]
        scores = lax.dot_general(q, keys, (((1,), (1,)), ((), ())), preferred_element_type=f32)
        where = chunk * local + lax.broadcasted_iota(jnp.int32, scores.shape, 1)
        allowed = where < length[0]
        scores = jnp.where(allowed, scores * SCALE, LOW)
        top = jnp.max(scores, axis=1, keepdims=True)
        weights = jnp.where(allowed, jnp.exp(scores - top), 0.0)
        total = jnp.sum(weights, axis=1, keepdims=True)
        mixed = jnp.dot(weights.astype(bf16), values, preferred_element_type=f32)
        lane = lax.broadcasted_iota(jnp.int32, (32, 128), 1)
        sums = jnp.zeros((32, 128), f32)
        for spot, piece in enumerate(thirds(top) + thirds(total)):
            sums = jnp.where(lane == spot, piece, sums)
        for which, piece in enumerate(thirds(mixed) + (sums,)):
            for half in range(2):
                lanes = slice((which * 2 + half) * 128, (which * 2 + half + 1) * 128)
                states[shift][:, lanes] = piece[16 * half : 16 * half + 16].astype(bf16)


def joined(parts):
    top = functools.reduce(jnp.maximum, [part[1] for part in parts])
    mixed, total = jnp.zeros_like(top), jnp.zeros_like(top)
    for part in parts:
        fade = jnp.exp(part[1] - top)
        mixed = mixed + part[0] * fade
        total = total + part[2] * fade
    return mixed, top, total


def shared(refs):
    lane = lax.broadcasted_iota(jnp.int32, (32, 128), 1)
    parts = []
    for ref in refs:
        blocks = [ref[:, i * 128 : (i + 1) * 128].astype(f32) for i in range(8)]
        mixed, sums = [
            jnp.concatenate(halves, axis=0)
            for halves in (
                [blocks[i] + blocks[i + 2] + blocks[i + 4] for i in range(2)],
                blocks[6:8],
            )
        ]
        top = jnp.sum(jnp.where(lane < 3, sums, 0.0), axis=1, keepdims=True)
        total = jnp.sum(jnp.where((lane >= 3) & (lane < 6), sums, 0.0), axis=1, keepdims=True)
        wide = [jnp.broadcast_to(value, (32, 128)) for value in (top, total)]
        parts.append([mixed] + wide)
    return jnp.concatenate(joined(parts), axis=0)


def state_kernel(q0, q1, q2, q3, out):
    out[...] = shared((q0, q1, q2, q3))


def project_kernel(for_keys, at, x0, x1, x2, x3, dec, gain, here, there, *rest):
    outs, (inputs, weights, product, result) = rest[:-4], rest[-4:]
    y, z, x, c, s = at[0], at[1], at[2], at[3], at[4]

    def arrange_weights(jy, carry):
        for jz in range(4):
            block = (((y - jy) & 3) * 4 + ((z - jz) & 3)) * 128
            for js in range(2):
                source = pl.ds(aligned(jy * 256 + jz * 64 + js * 32, 32), 32)
                place = block + (s ^ js) * 32
                weights[pl.ds(aligned(place + c * 64, 32), 32), :] = here[source, :]
                weights[pl.ds(aligned(place + (1 - c) * 64, 32), 32), :] = there[source, :]
        return carry

    lax.fori_loop(0, 4, arrange_weights, 0)
    pieces = [(x0, x & 3, CHUNK), (x1, (x - 1) & 3, CHUNK), (x2, (x - 2) & 3, CHUNK)]
    pieces += [(x3, (x - 3) & 3, CHUNK), (dec, 4, 16)]

    def split(block):
        columns = pl.ds(aligned(block * 128, 128), 128)
        factor = gain[:, pl.ds(aligned(block * 512 + x * 128, 128), 128)]
        for ref, position, count in pieces:
            start = position * CHUNK
            value = ref[:, columns].astype(f32) * factor
            high = value.astype(bf16)
            inputs[pl.ds(aligned(start, 16), count), columns] = high
            if for_keys:
                inputs[pl.ds(aligned(start + ROWS, 16), count), columns] = (
                    value - high.astype(f32)
                ).astype(bf16)

    def split_some(group, carry):
        for part in range(4):
            split(group * 4 + part)
        return carry

    lax.fori_loop(0, 4, split_some, 0)
    height = ROWS if for_keys else ROWS // 3

    def multiply(part, carry):
        rows = pl.ds(aligned(part * height, 16), height)
        product[rows, :] = jnp.dot(inputs[rows, :], weights[...], preferred_element_type=f32)
        return carry

    lax.fori_loop(0, 2 if for_keys else 3, multiply, 0)
    for ref, position, count in pieces:
        start = position * CHUNK
        tail = ref[:, SLICE:].astype(f32)
        lane = lax.broadcasted_iota(jnp.int32, tail.shape, 1)
        factor = jnp.sum(jnp.where(lane < 3, tail, 0.0), axis=1, keepdims=True)
        rows = pl.ds(aligned(start, 16), count)
        value = product[rows, :]
        if for_keys:
            value = value + product[pl.ds(aligned(start + ROWS, 16), count), :]
        result[rows, :] = value * factor
    for shift in range(4):
        head = (x + shift) & 3
        outs[shift][...] = result[:, pl.ds(aligned(head * 128, 128), 128)].astype(
            outs[shift].dtype
        )
    if for_keys:
        outs[4][...] = jnp.zeros((16, 128), f32)
        for ref, position, _ in pieces[:4]:
            tail = ref[:, SLICE:].astype(f32)
            lane = lax.broadcasted_iota(jnp.int32, tail.shape, 1)
            seg = jnp.sum(jnp.where(lane == 3, tail, 0.0), axis=1, keepdims=True)
            spread = jnp.broadcast_to(seg, (128, 128))
            outs[4][pl.ds(position, 1), :] = jnp.sum(
                jnp.where(diagonal(), spread, 0.0), axis=0, keepdims=True
            )


def keys_kernel(k0, k1, k2, k3, seg, slab, dec_key):
    key = (k0[...] + k1[...]) + (k2[...] + k3[...])
    scaled = key[: 4 * CHUNK] * FACTOR
    high = scaled.astype(bf16)
    slab[0 : 4 * CHUNK, 0:128] = high
    slab[0 : 4 * CHUNK, 128:256] = (scaled - high.astype(f32)).astype(bf16)
    slab[4 * CHUNK : ROWS, 0:128] = seg[...].astype(bf16)
    slab[4 * CHUNK : ROWS, 128:256] = jnp.zeros((16, 128), bf16)
    dec_key[...] = key[4 * CHUNK :]


def values_kernel(v0, v1, v2, v3, slab, dec_value):
    value = (v0[...] + v1[...].astype(f32)) + (v2[...].astype(f32) + v3[...].astype(f32))
    slab[...] = value[: 4 * CHUNK].astype(bf16)
    dec_value[...] = value[4 * CHUNK :]


def load_keys(keys, values, slabs, segs, ends):
    for side in range(2):
        for a in range(4):
            rows, chunk = slice(side * 128, side * 128 + 128), slice(a * 128, a * 128 + 128)
            slabs[a, rows, 0:256] = keys[side][chunk, :]
            slabs[a, rows, 256:384] = values[side][chunk, :]
        segs[16 * side : 16 * side + 16, :] = keys[side][4 * CHUNK : ROWS, 0:128].astype(f32)
    for a in range(4):
        ends[a] = jnp.max(jnp.maximum(segs[a : a + 1, :], segs[16 + a : 17 + a, :]))


def double(query, q):
    for group in range(8):
        piece = query[0:CHUNK, group * 128 : (group + 1) * 128]
        q[group * 128 : (group + 1) * 128, 0:128] = piece
        q[group * 128 : (group + 1) * 128, 128:256] = piece


def attend(a, chunk, place, pair, column, q, slabs, segs, top, total, mixed):
    keys = slabs[a, :, 0:256]
    values = slabs[a, :, 256:384]
    rows = lax.broadcasted_iota(jnp.int32, (128, 128), 0)
    lanes = lax.broadcasted_iota(jnp.int32, (128, 128), 1)

    def bias(side):
        seg = segs[pl.ds(16 * side + a, 1), :]
        where = place ^ (pair + 2 * side)
        allowed = (column == seg) & (
            a * 512 + where * 128 + lanes <= chunk * 512 + place * 128 + rows
        )
        return jnp.where(allowed, 0.0, LOW)[None]

    biases = bias(0), bias(1)

    def half(part, carry):
        some = pl.ds(aligned(part * 512, 128), 512)
        scores = lax.dot_general(
            q[some, :], keys, (((1,), (1,)), ((), ())), preferred_element_type=f32
        )
        left, right = [
            (scores[:, side * 128 : side * 128 + 128].reshape(4, 128, 128) + biases[side]).reshape(
                512, 128
            )
            for side in range(2)
        ]
        highest = jnp.max(jnp.maximum(left, right), axis=1, keepdims=True)
        before = top[some, :]
        after = jnp.maximum(before, highest)
        fade = jnp.exp2(before - after)
        left = jnp.exp2(left - after)
        right = jnp.exp2(right - after)
        top[some, :] = after
        total[some, :] = total[some, :] * fade + (left + right)
        weights = jnp.concatenate([left.astype(bf16), right.astype(bf16)], axis=1)
        mixed[some, :] = mixed[some, :] * fade + jnp.dot(
            weights, values, preferred_element_type=f32
        )
        return carry

    lax.fori_loop(0, 2, half, 0)


def near_kernel(
    at, q0, q1, q2, q3, own, other_c, own_value, other_value, seg,
    top, total, mixed, slabs, q, segs, ends,
):
    x, place = at[2], at[3] * 2 + at[4]
    load_keys((own, other_c), (own_value, other_value), slabs, segs, ends)
    for shift, query in enumerate((q0, q3, q2, q1)):
        double(query, q.at[shift])
    top[...] = jnp.full(top.shape, LOW, f32)
    total[...] = jnp.zeros(total.shape, f32)
    mixed[...] = jnp.zeros(mixed.shape, f32)

    def query_chunk(shift, carry):
        chunk = (x + shift) & 3
        row = seg[pl.ds(chunk, 1), :]
        column = column_of(row)
        first = jnp.min(row)
        state = (q.at[shift], slabs, segs, top.at[shift], total.at[shift], mixed.at[shift])

        def step(back, inner):
            a = chunk - back

            @pl.when((back == 0) | (ends[a] >= first))
            def _():
                attend(a, chunk, place, 0, column, *state)

            return inner

        lax.fori_loop(0, chunk + 1, step, 0)
        return carry

    lax.fori_loop(0, 4, query_chunk, 0)


def far_kernel(
    shift, at, query, other_s, other_both, value_s, value_both, seg, rollout, top0, total0, mixed0,
    out, slabs, q, segs, ends, top, total, mixed,
):
    x, place = at[2], at[3] * 2 + at[4]
    chunk = (x + shift) & 3
    load_keys((other_s, other_both), (value_s, value_both), slabs, segs, ends)
    double(query, q)
    top[...] = top0[shift]
    total[...] = total0[shift]
    mixed[...] = mixed0[shift]
    row = seg[pl.ds(chunk, 1), :]
    column = column_of(row)
    first = jnp.min(row)
    state = (q, slabs, segs, top, total, mixed)

    def step(a, carry):
        @pl.when(((a < chunk) | (place > 0)) & (ends[a] >= first))
        def _():
            attend(a, chunk, place, 1, column, *state)

        return carry

    lax.fori_loop(0, chunk + 1, step, 0)
    sums = jnp.sum(total[...], axis=1, keepdims=True)
    for group in range(8):
        piece = slice(group * 128, (group + 1) * 128)
        out[0:CHUNK, piece] = (mixed[piece, :] / sums[piece, :]).astype(bf16)
    out[CHUNK:, :] = rollout[...]


def rollout_kernel(at, query, s0, s1, s2, s3, key, value, out, rows):
    head = at[2]
    for group in range(8):
        start = aligned(head * 1024 + group * 128, 128)
        rows[group * 4 : group * 4 + 4, :] = query[:, pl.ds(start, 128)].astype(f32)
    q = rows[...]
    step = lax.broadcasted_iota(jnp.int32, (32, 128), 0) & 3
    scores = []
    for j in range(STEPS):
        score = jnp.sum(q * key[j : j + 1, :], axis=1, keepdims=True) * SCALE
        scores.append(jnp.where(step >= j, jnp.broadcast_to(score, (32, 128)), LOW))
    mixed, top, total = joined(
        [[ref[32 * i : 32 * i + 32, :] for i in range(3)] for ref in (s0, s1, s2, s3)]
    )
    high = functools.reduce(jnp.maximum, scores, top)
    fade = jnp.exp(top - high)
    mixed, total = mixed * fade, total * fade
    for j, score in enumerate(scores):
        weight = jnp.where(step >= j, jnp.exp(score - high), 0.0)
        total = total + weight
        mixed = mixed + weight.astype(bf16).astype(f32) * value[j : j + 1, :]
    rows[...] = mixed / total
    out[...] = jnp.zeros(out.shape, bf16)
    for group in range(8):
        out[0:4, group * 128 : (group + 1) * 128] = rows[group * 4 : group * 4 + 4, :].astype(bf16)


def arrange_kernel(at, p0, p1, p2, p3, pack, dec):
    x = at[2]
    for shift, part in enumerate((p0, p1, p2, p3)):
        start = aligned(((x - shift) & 3) * 1024, 128)
        pack[:, pl.ds(start, 1024)] = part[0:CHUNK, :]
        dec[:, pl.ds(start, 1024)] = part[CHUNK : CHUNK + STEPS, :]


def moved(value, axis, shift):
    size = 2 if axis in ("c", "s") else 4
    return lax.ppermute(value, axis, [(i, (i + shift) % size) for i in range(size)])


def around(values, axis):
    return [values[0]] + [moved(values[i], axis, i) for i in (1, 2, 3)]


def layer(
    dec_in,
    decode_query,
    cache,
    ctx_len,
    pack_in,
    packed_query,
    seg_ids,
    norm_gain,
    key_value_weight,
):
    at = jnp.stack([lax.axis_index(name) for name in ("y", "zl", "x", "c", "s")]).astype(jnp.int32)
    dec_query = decode_query[0]
    gain = norm_gain.reshape(1, WIDTH)

    weight = jnp.concatenate([key_value_weight, moved(key_value_weight, "s", 1)], axis=0)
    *messages, dec_message = call(
        prepare_kernel,
        [sds((CHUNK, MESSAGE), bf16)] * 4 + [sds((16, MESSAGE), bf16)],
        (at, pack_in, seg_ids.reshape(1, CHUNK), dec_in[0]),
        scratch=[pltpu.VMEM((16, WIDTH), f32)],
    )
    inputs = around(messages, "x")
    cached = call(
        cache_kernel,
        [sds((CHUNK, 1024), bf16)] * 4 + [sds((16, 1024), bf16)] * 4,
        (at, ctx_len, dec_query, cache[0], packed_query),
        smem=2,
        scratch=[pltpu.VMEM((32, 128), f32)],
    )
    queries = around(cached[:4], "x")

    def gathered(part):
        part = jnp.concatenate(around([part] * 4, "zl"), axis=0)
        part = jnp.concatenate(around([part] * 4, "y"), axis=0)
        return part, moved(part, "c", 1)

    key_weight = gathered(weight[:, :512])
    value_weight = gathered(weight[:, 512:])

    def projected(part, kind, form):
        for_keys = kind == "k"
        height = 2 * ROWS if for_keys else ROWS
        outs = call(
            functools.partial(project_kernel, for_keys),
            [sds((ROWS, 128), f32)]
            + [sds((ROWS, 128), form)] * 3
            + [sds((16, 128), f32)] * for_keys,
            (at, *inputs, dec_message, gain, *part),
            scratch=[
                pltpu.VMEM((height, SLICE), bf16),
                pltpu.VMEM((SLICE, 512), bf16),
                pltpu.VMEM((height, 512), f32),
                pltpu.VMEM((ROWS, 512), f32),
            ],
        )
        return around(outs[:4], "x"), outs[4:]

    keys, (seg,) = projected(key_weight, "k", f32)
    values, _ = projected(value_weight, "v", bf16)

    state = call(state_kernel, sds((96, 128), f32), around(cached[4:], "x"), smem=0)
    state_s = moved(state, "s", 1)
    states = [state, state_s, moved(state, "c", 1), moved(state_s, "c", 1)]

    key, dec_key = call(
        keys_kernel, [sds((ROWS, 256), bf16), sds((16, 128), f32)], (*keys, seg), smem=0
    )
    key_s = moved(key, "s", 1)
    key_c = moved(key, "c", 1)
    value, dec_value = call(
        values_kernel, [sds((4 * CHUNK, 128), bf16), sds((16, 128), f32)], values, smem=0
    )
    value_s = moved(value, "s", 1)
    value_c = moved(value, "c", 1)
    slots = [
        pltpu.VMEM((4, 256, 384), bf16),
        pltpu.VMEM((4, 1024, 256), bf16),
        pltpu.VMEM((32, 128), f32),
        pltpu.SMEM((4,), f32),
    ]
    running = call(
        near_kernel,
        [sds((4, 1024, 128), f32)] * 3,
        (at, *queries, key, key_c, value, value_c, seg),
        scratch=slots,
    )
    key_both = moved(key_s, "c", 1)
    value_both = moved(value_s, "c", 1)
    rollout = call(
        rollout_kernel,
        sds((8, 1024), bf16),
        (at, dec_query, *states, dec_key, dec_value),
        scratch=[pltpu.VMEM((32, 128), f32)],
    )
    slots[1] = pltpu.VMEM((1024, 256), bf16)
    parts = [None] * 4
    for shift in (2, 1, 3, 0):
        part = call(
            functools.partial(far_kernel, shift),
            sds((CHUNK + 8, 1024), bf16),
            (
                at, queries[(4 - shift) % 4], key_s, key_both, value_s, value_both, seg, rollout,
                *running,
            ),
            scratch=slots + [pltpu.VMEM((1024, 128), f32)] * 3,
        )
        parts[shift] = part if shift == 0 else moved(part, "x", shift)
    pack_out, dec_out = call(
        arrange_kernel, [sds((CHUNK, 4096), bf16), sds((STEPS, 4096), bf16)], (at, *parts)
    )
    return dec_out[None], pack_out


def solution(mesh):
    grid = Mesh(mesh.devices.reshape(4, 4, 4, 2, 2), ("y", "zl", "x", "c", "s"))
    rep = ("y", "zl")
    rest = ("x", "c", "s")
    placed = (
        P(rep, None, None),
        P(rep, None, None),
        P(rep, rest, None),
        P(rep),
        P(rep + rest, None),
        P(rep + rest, None),
        P(rep + rest),
        P(),
        P(rep + rest, None),
    )
    return jax.shard_map(
        layer,
        mesh=grid,
        in_specs=placed,
        out_specs=(P(rep, None, None), P(rep + rest, None)),
        check_vma=False,
    )
```

```python
import functools
import math

import jax
import jax.numpy as jnp
from jax import lax
from jax.experimental import pallas as pl
from jax.experimental.pallas import tpu as pltpu
from jax.sharding import Mesh
from jax.sharding import PartitionSpec as P


WIDTH = 8192
HEAD = 128
STEPS = 4
CHUNK = 128
SLICE = 2048
MESSAGE = SLICE + 128
ROWS = 4 * CHUNK + 16
FACTOR = math.log2(math.e) / math.sqrt(HEAD)
SCALE = 1.0 / math.sqrt(HEAD)
LOW = -1e30

f32 = jnp.float32
bf16 = jnp.bfloat16


VMEM = pl.BlockSpec(memory_space=pltpu.VMEM)
SMEM = pl.BlockSpec(memory_space=pltpu.SMEM)


def call(body, outs, inputs, smem=1, scratch=()):
    inputs = [
        value if i < smem else pltpu.with_memory_space_constraint(value, pltpu.VMEM)
        for i, value in enumerate(inputs)
    ]
    return pl.pallas_call(
        body,
        out_shape=outs,
        in_specs=[SMEM] * smem + [VMEM] * (len(inputs) - smem),
        out_specs=jax.tree.map(lambda _: VMEM, outs),
        scratch_shapes=list(scratch),
        compiler_params=pltpu.CompilerParams(vmem_limit_bytes=32 * 1024 * 1024),
    )(*inputs)


def sds(shape, dtype):
    return jax.ShapeDtypeStruct(shape, dtype)


def aligned(value, multiple):
    return pl.multiple_of(value, multiple)


def columns_of(ref, rows, seg):
    power = jnp.zeros((rows, 128), f32)
    for block in range(WIDTH // 128):
        piece = ref[:, block * 128 : (block + 1) * 128].astype(f32)
        power = power + piece * piece
    mean = jnp.sum(power, axis=1, keepdims=True) * (1.0 / WIDTH)
    factor = lax.rsqrt(mean + 1e-05)
    high, middle, low = thirds(factor)
    lane = lax.broadcasted_iota(jnp.int32, (rows, 128), 1)
    packed = jnp.where(
        lane == 0, high, jnp.where(lane == 1, middle, jnp.where(lane == 2, low, 0.0))
    )
    if seg is not None:
        packed = jnp.where(lane == 3, seg, packed)
    return packed.astype(bf16)


def thirds(value):
    high = value.astype(bf16).astype(f32)
    middle = (value - high).astype(bf16).astype(f32)
    return high, middle, value - high - middle


def diagonal():
    rows = lax.broadcasted_iota(jnp.int32, (128, 128), 0)
    return rows == lax.broadcasted_iota(jnp.int32, (128, 128), 1)


def column_of(row):
    spread = jnp.broadcast_to(row, (128, 128))
    return jnp.sum(jnp.where(diagonal(), spread, 0.0), axis=1, keepdims=True)


def prepare_kernel(at, pack, seg, rollout, *outs):
    x = at[2]
    messages, dec_message, dec = outs[:4], outs[4], outs[5]
    dec[...] = jnp.zeros(dec.shape, f32)
    dec[0:STEPS, :] = rollout[...].astype(f32)
    columns = columns_of(pack, CHUNK, column_of(seg[...].astype(f32)))
    for shift in range(4):
        target = (x + shift) & 3
        for block in range(16):
            start = aligned(block * 512 + target * 128, 128)
            messages[shift][:, block * 128 : (block + 1) * 128] = pack[:, pl.ds(start, 128)]
        messages[shift][:, SLICE:] = columns
    for block in range(16):
        start = aligned(block * 512 + x * 128, 128)
        dec_message[:, block * 128 : (block + 1) * 128] = dec[:, pl.ds(start, 128)].astype(bf16)
    dec_message[:, SLICE:] = columns_of(dec, 16, None)


def cache_kernel(at, length, query, cache, packed, *rest):
    outs, rows = rest[:4], rest[4]
    x, chunk = at[2], at[2] * 4 + at[3] * 2 + at[4]
    local = cache.shape[0]
    for shift in range(4):
        head = (x + shift) & 3
        out = outs[shift]
        out[0:CHUNK, :] = packed[:, pl.ds(aligned(head * 1024, 128), 1024)]
        for group in range(8):
            start = aligned(head * 1024 + group * 128, 128)
            rows[group * 4 : group * 4 + 4, :] = query[:, pl.ds(start, 128)].astype(f32)
        q = rows[...].astype(bf16)
        keys = cache[:, pl.ds(aligned(head * 128, 128), 128)]
        values = cache[:, pl.ds(aligned(512 + head * 128, 128), 128)]
        scores = lax.dot_general(q, keys, (((1,), (1,)), ((), ())), preferred_element_type=f32)
        where = chunk * local + lax.broadcasted_iota(jnp.int32, scores.shape, 1)
        allowed = where < length[0]
        scores = jnp.where(allowed, scores * SCALE, LOW)
        top = jnp.max(scores, axis=1, keepdims=True)
        weights = jnp.where(allowed, jnp.exp(scores - top), 0.0)
        total = jnp.sum(weights, axis=1, keepdims=True)
        mixed = jnp.dot(weights.astype(bf16), values, preferred_element_type=f32)
        for spot, block in enumerate(compact(mixed, top, total)):
            out[CHUNK:, spot * 128 : (spot + 1) * 128] = block


def compact(mixed, top, total):
    lane = lax.broadcasted_iota(jnp.int32, (32, 128), 1)
    sums = jnp.zeros((32, 128), f32)
    for spot, piece in enumerate(thirds(top) + thirds(total)):
        sums = jnp.where(lane == spot, piece, sums)
    return [
        piece[16 * half : 16 * half + 16].astype(bf16)
        for piece in thirds(mixed) + (sums,)
        for half in range(2)
    ]


def expanded(blocks):
    lane = lax.broadcasted_iota(jnp.int32, (32, 128), 1)
    blocks = [block.astype(f32) for block in blocks]
    mixed = jnp.concatenate([blocks[i] + blocks[i + 2] + blocks[i + 4] for i in range(2)], axis=0)
    sums = jnp.concatenate(blocks[6:8], axis=0)
    top = jnp.sum(jnp.where(lane < 3, sums, 0.0), axis=1, keepdims=True)
    total = jnp.sum(jnp.where((lane >= 3) & (lane < 6), sums, 0.0), axis=1, keepdims=True)
    return [mixed, jnp.broadcast_to(top, (32, 128)), jnp.broadcast_to(total, (32, 128))]


def joined(parts):
    top = functools.reduce(jnp.maximum, [part[1] for part in parts])
    mixed, total = jnp.zeros_like(top), jnp.zeros_like(top)
    for part in parts:
        fade = jnp.exp(part[1] - top)
        mixed = mixed + part[0] * fade
        total = total + part[2] * fade
    return mixed, top, total


def shared(refs):
    return joined(
        [expanded([ref[CHUNK:, i * 128 : (i + 1) * 128] for i in range(8)]) for ref in refs]
    )


def state_place(spot):
    row, lane = ROWS + 16 * (spot // 2), 128 * (spot % 2)
    return slice(row, row + 16), slice(lane, lane + 128)


def project_kernel(for_keys, at, x0, x1, x2, x3, dec, gain, here, there, *rest):
    outs, (inputs, weights, product, result) = rest[:-4], rest[-4:]
    y, z, x, c, s = at[0], at[1], at[2], at[3], at[4]
    for jy in range(4):
        for jz in range(4):
            block = (((y - jy) & 3) * 4 + ((z - jz) & 3)) * 128
            for js in range(2):
                source = (jy * 4 + jz) * 64 + js * 32
                place = block + (s ^ js) * 32
                weights[pl.ds(aligned(place + c * 64, 32), 32), :] = here[source : source + 32, :]
                weights[pl.ds(aligned(place + (1 - c) * 64, 32), 32), :] = there[
                    source : source + 32, :
                ]
    pieces = [(x0, x & 3, CHUNK), (x1, (x - 1) & 3, CHUNK), (x2, (x - 2) & 3, CHUNK)]
    pieces += [(x3, (x - 3) & 3, CHUNK), (dec, 4, 16)]
    for block in range(16):
        columns = slice(block * 128, (block + 1) * 128)
        factor = gain[:, pl.ds(aligned(block * 512 + x * 128, 128), 128)]
        for ref, position, count in pieces:
            start = position * CHUNK
            value = ref[:, columns].astype(f32) * factor
            high = value.astype(bf16)
            inputs[pl.ds(aligned(start, 16), count), columns] = high
            if for_keys:
                inputs[pl.ds(aligned(start + ROWS, 16), count), columns] = (
                    value - high.astype(f32)
                ).astype(bf16)
    product[...] = jnp.dot(inputs[...], weights[...], preferred_element_type=f32)
    for ref, position, count in pieces:
        start = position * CHUNK
        tail = ref[:, SLICE:].astype(f32)
        lane = lax.broadcasted_iota(jnp.int32, tail.shape, 1)
        factor = jnp.sum(jnp.where(lane < 3, tail, 0.0), axis=1, keepdims=True)
        rows = pl.ds(aligned(start, 16), count)
        value = product[rows, :]
        if for_keys:
            value = value + product[pl.ds(aligned(start + ROWS, 16), count), :]
        result[rows, :] = value * factor
    for shift in range(4):
        head = (x + shift) & 3
        outs[shift][...] = result[:, pl.ds(aligned(head * 128, 128), 128)].astype(
            outs[shift].dtype
        )
    if for_keys:
        outs[4][...] = jnp.zeros((16, 128), f32)
        for ref, position, _ in pieces[:4]:
            tail = ref[:, SLICE:].astype(f32)
            lane = lax.broadcasted_iota(jnp.int32, tail.shape, 1)
            seg = jnp.sum(jnp.where(lane == 3, tail, 0.0), axis=1, keepdims=True)
            spread = jnp.broadcast_to(seg, (128, 128))
            outs[4][pl.ds(position, 1), :] = jnp.sum(
                jnp.where(diagonal(), spread, 0.0), axis=0, keepdims=True
            )


def keys_kernel(k0, k1, k2, k3, seg, q0, q1, q2, q3, slab, dec_key):
    for spot, block in enumerate(compact(*shared((q0, q1, q2, q3)))):
        slab[state_place(spot)] = block
    key = (k0[...] + k1[...]) + (k2[...] + k3[...])
    scaled = key[: 4 * CHUNK] * FACTOR
    high = scaled.astype(bf16)
    slab[0 : 4 * CHUNK, 0:128] = high
    slab[0 : 4 * CHUNK, 128:256] = (scaled - high.astype(f32)).astype(bf16)
    slab[4 * CHUNK : ROWS, 0:128] = seg[...].astype(bf16)
    slab[4 * CHUNK : ROWS, 128:256] = jnp.zeros((16, 128), bf16)
    dec_key[...] = key[4 * CHUNK :]


def values_kernel(v0, v1, v2, v3, slab, dec_value):
    value = (v0[...] + v1[...].astype(f32)) + (v2[...].astype(f32) + v3[...].astype(f32))
    slab[...] = value[: 4 * CHUNK].astype(bf16)
    dec_value[...] = value[4 * CHUNK :]


def load_keys(keys, values, slabs, segs, ends):
    for side in range(2):
        for a in range(4):
            rows, chunk = slice(side * 128, side * 128 + 128), slice(a * 128, a * 128 + 128)
            slabs[a, rows, 0:256] = keys[side][chunk, :]
            slabs[a, rows, 256:384] = values[side][chunk, :]
        segs[16 * side : 16 * side + 16, :] = keys[side][4 * CHUNK : ROWS, 0:128].astype(f32)
    for a in range(4):
        ends[a] = jnp.max(jnp.maximum(segs[a : a + 1, :], segs[16 + a : 17 + a, :]))


def double(query, q):
    for group in range(8):
        piece = query[0:CHUNK, group * 128 : (group + 1) * 128]
        q[group * 128 : (group + 1) * 128, 0:128] = piece
        q[group * 128 : (group + 1) * 128, 128:256] = piece


def attend(a, chunk, place, pair, column, q, slabs, segs, top, total, mixed):
    keys = slabs[a, :, 0:256]
    values = slabs[a, :, 256:384]
    scores = lax.dot_general(q[...], keys, (((1,), (1,)), ((), ())), preferred_element_type=f32)
    rows = lax.broadcasted_iota(jnp.int32, (128, 128), 0)
    lanes = lax.broadcasted_iota(jnp.int32, (128, 128), 1)

    def hidden(score, side):
        seg = segs[pl.ds(16 * side + a, 1), :]
        where = place ^ (pair + 2 * side)
        allowed = (column == seg) & (
            a * 512 + where * 128 + lanes <= chunk * 512 + place * 128 + rows
        )
        bias = jnp.where(allowed, 0.0, LOW)
        return (score.reshape(8, 128, 128) + bias[None]).reshape(1024, 128)

    left, right = hidden(scores[:, 0:128], 0), hidden(scores[:, 128:256], 1)
    highest = jnp.max(jnp.maximum(left, right), axis=1, keepdims=True)
    before = top[...]
    after = jnp.maximum(before, highest)
    fade = jnp.exp2(before - after)
    left = jnp.exp2(left - after)
    right = jnp.exp2(right - after)
    top[...] = after
    total[...] = total[...] * fade + (left + right)
    weights = jnp.concatenate([left.astype(bf16), right.astype(bf16)], axis=1)
    mixed[...] = mixed[...] * fade + jnp.dot(weights, values, preferred_element_type=f32)


def near_kernel(
    at, q0, q1, q2, q3, own, other_c, own_value, other_value, seg,
    top, total, mixed, slabs, q, segs, ends,
):
    x, place = at[2], at[3] * 2 + at[4]
    load_keys((own, other_c), (own_value, other_value), slabs, segs, ends)
    for shift, query in enumerate((q0, q3, q2, q1)):
        double(query, q.at[shift])
    top[...] = jnp.full(top.shape, LOW, f32)
    total[...] = jnp.zeros(total.shape, f32)
    mixed[...] = jnp.zeros(mixed.shape, f32)

    def query_chunk(shift, carry):
        chunk = (x + shift) & 3
        row = seg[pl.ds(chunk, 1), :]
        column = column_of(row)
        first = jnp.min(row)
        state = (q.at[shift], slabs, segs, top.at[shift], total.at[shift], mixed.at[shift])

        def step(back, inner):
            a = chunk - back

            @pl.when((back == 0) | (ends[a] >= first))
            def _():
                attend(a, chunk, place, 0, column, *state)

            return inner

        lax.fori_loop(0, chunk + 1, step, 0)
        return carry

    lax.fori_loop(0, 4, query_chunk, 0)


def far_kernel(
    shift, at, query, other_s, other_both, value_s, value_both, seg, rollout, top0, total0, mixed0,
    out, slabs, q, segs, ends, top, total, mixed,
):
    x, place = at[2], at[3] * 2 + at[4]
    chunk = (x + shift) & 3
    load_keys((other_s, other_both), (value_s, value_both), slabs, segs, ends)
    double(query, q)
    top[...] = top0[shift]
    total[...] = total0[shift]
    mixed[...] = mixed0[shift]
    row = seg[pl.ds(chunk, 1), :]
    column = column_of(row)
    first = jnp.min(row)
    state = (q, slabs, segs, top, total, mixed)

    def step(a, carry):
        @pl.when(((a < chunk) | (place > 0)) & (ends[a] >= first))
        def _():
            attend(a, chunk, place, 1, column, *state)

        return carry

    lax.fori_loop(0, chunk + 1, step, 0)
    sums = jnp.sum(total[...], axis=1, keepdims=True)
    for group in range(8):
        piece = slice(group * 128, (group + 1) * 128)
        out[0:CHUNK, piece] = (mixed[piece, :] / sums[piece, :]).astype(bf16)
    out[CHUNK:, :] = rollout[...]


def rollout_kernel(at, query, s0, s1, s2, s3, key, value, out, rows):
    head = at[2]
    for group in range(8):
        start = aligned(head * 1024 + group * 128, 128)
        rows[group * 4 : group * 4 + 4, :] = query[:, pl.ds(start, 128)].astype(f32)
    q = rows[...]
    step = lax.broadcasted_iota(jnp.int32, (32, 128), 0) & 3
    scores = []
    for j in range(STEPS):
        score = jnp.sum(q * key[j : j + 1, :], axis=1, keepdims=True) * SCALE
        scores.append(jnp.where(step >= j, jnp.broadcast_to(score, (32, 128)), LOW))
    mixed, top, total = joined(
        [expanded([slab[state_place(i)] for i in range(8)]) for slab in (s0, s1, s2, s3)]
    )
    high = functools.reduce(jnp.maximum, scores, top)
    fade = jnp.exp(top - high)
    mixed, total = mixed * fade, total * fade
    for j, score in enumerate(scores):
        weight = jnp.where(step >= j, jnp.exp(score - high), 0.0)
        total = total + weight
        mixed = mixed + weight.astype(bf16).astype(f32) * value[j : j + 1, :]
    rows[...] = mixed / total
    out[...] = jnp.zeros(out.shape, bf16)
    for group in range(8):
        out[0:4, group * 128 : (group + 1) * 128] = rows[group * 4 : group * 4 + 4, :].astype(bf16)


def arrange_kernel(at, p0, p1, p2, p3, pack, dec):
    x = at[2]
    for shift, part in enumerate((p0, p1, p2, p3)):
        start = aligned(((x - shift) & 3) * 1024, 128)
        pack[:, pl.ds(start, 1024)] = part[0:CHUNK, :]
        dec[:, pl.ds(start, 1024)] = part[CHUNK : CHUNK + STEPS, :]


def moved(value, axis, shift):
    size = 2 if axis in ("c", "s") else 4
    return lax.ppermute(value, axis, [(i, (i + shift) % size) for i in range(size)])


def around(values, axis):
    return [values[0]] + [moved(values[i], axis, i) for i in (1, 2, 3)]


def layer(
    dec_in,
    decode_query,
    cache,
    ctx_len,
    pack_in,
    packed_query,
    seg_ids,
    norm_gain,
    key_value_weight,
):
    at = jnp.stack([lax.axis_index(name) for name in ("y", "zl", "x", "c", "s")]).astype(jnp.int32)
    dec_query = decode_query[0]
    gain = norm_gain.reshape(1, WIDTH)

    weight = jnp.concatenate([key_value_weight, moved(key_value_weight, "s", 1)], axis=0)
    *messages, dec_message = call(
        prepare_kernel,
        [sds((CHUNK, MESSAGE), bf16)] * 4 + [sds((16, MESSAGE), bf16)],
        (at, pack_in, seg_ids.reshape(1, CHUNK), dec_in[0]),
        scratch=[pltpu.VMEM((16, WIDTH), f32)],
    )
    inputs = around(messages, "x")
    weight = jnp.concatenate(around([weight] * 4, "zl"), axis=0)
    cached = call(
        cache_kernel,
        [sds((CHUNK + 16, 1024), bf16)] * 4,
        (at, ctx_len, dec_query, cache[0], packed_query),
        smem=2,
        scratch=[pltpu.VMEM((32, 128), f32)],
    )
    queries = around(cached, "x")

    def gathered(part):
        part = jnp.concatenate(around([part] * 4, "y"), axis=0)
        return part, moved(part, "c", 1)

    key_weight = gathered(weight[:, :512])
    value_weight = gathered(weight[:, 512:])

    def projected(part, kind, form):
        for_keys = kind == "k"
        height = 2 * ROWS if for_keys else ROWS
        outs = call(
            functools.partial(project_kernel, for_keys),
            [sds((ROWS, 128), f32)]
            + [sds((ROWS, 128), form)] * 3
            + [sds((16, 128), f32)] * for_keys,
            (at, *inputs, dec_message, gain, *part),
            scratch=[
                pltpu.VMEM((height, SLICE), bf16),
                pltpu.VMEM((SLICE, 512), bf16),
                pltpu.VMEM((height, 512), f32),
                pltpu.VMEM((ROWS, 512), f32),
            ],
        )
        return around(outs[:4], "x"), outs[4:]

    keys, (seg,) = projected(key_weight, "k", f32)
    values, _ = projected(value_weight, "v", bf16)

    key, dec_key = call(
        keys_kernel,
        [sds((ROWS + 64, 256), bf16), sds((16, 128), f32)],
        (*keys, seg, *queries),
        smem=0,
    )
    key_s = moved(key, "s", 1)
    key_c = moved(key, "c", 1)
    value, dec_value = call(
        values_kernel, [sds((4 * CHUNK, 128), bf16), sds((16, 128), f32)], values, smem=0
    )
    value_s = moved(value, "s", 1)
    value_c = moved(value, "c", 1)
    slots = [
        pltpu.VMEM((4, 256, 384), bf16),
        pltpu.VMEM((4, 1024, 256), bf16),
        pltpu.VMEM((32, 128), f32),
        pltpu.SMEM((4,), f32),
    ]
    running = call(
        near_kernel,
        [sds((4, 1024, 128), f32)] * 3,
        (at, *queries, key, key_c, value, value_c, seg),
        scratch=slots,
    )
    key_both = moved(key_s, "c", 1)
    value_both = moved(value_s, "c", 1)
    rollout = call(
        rollout_kernel,
        sds((8, 1024), bf16),
        (at, dec_query, key, key_s, key_c, key_both, dec_key, dec_value),
        scratch=[pltpu.VMEM((32, 128), f32)],
    )
    slots[1] = pltpu.VMEM((1024, 256), bf16)
    parts = [None] * 4
    for shift in (2, 1, 3, 0):
        part = call(
            functools.partial(far_kernel, shift),
            sds((CHUNK + 8, 1024), bf16),
            (
                at, queries[(4 - shift) % 4], key_s, key_both, value_s, value_both, seg, rollout,
                *running,
            ),
            scratch=slots + [pltpu.VMEM((1024, 128), f32)] * 3,
        )
        parts[shift] = part if shift == 0 else moved(part, "x", shift)
    pack_out, dec_out = call(
        arrange_kernel, [sds((CHUNK, 4096), bf16), sds((STEPS, 4096), bf16)], (at, *parts)
    )
    return dec_out[None], pack_out


def solution(mesh):
    grid = Mesh(mesh.devices.reshape(4, 4, 4, 2, 2), ("y", "zl", "x", "c", "s"))
    rep = ("y", "zl")
    rest = ("x", "c", "s")
    placed = (
        P(rep, None, None),
        P(rep, None, None),
        P(rep, rest, None),
        P(rep),
        P(rep + rest, None),
        P(rep + rest, None),
        P(rep + rest),
        P(),
        P(rep + rest, None),
    )
    return jax.shard_map(
        layer,
        mesh=grid,
        in_specs=placed,
        out_specs=(P(rep, None, None), P(rep + rest, None)),
        check_vma=False,
    )
```
